32 devices in a mesh: seq: 16 (over z, y, x), mp: 2 (over core).
Axes of the slice: x: 2, y: 2, z: 4, core: 2. Of those that a mesh axis runs over, the one named last changes fastest.
Arguments:
- layer_input: float32 [4096, 1024], P('seq'), may hold values from -6 to 6
- cotangent: float32 [4096, 1024], P('seq'), may hold values from -6 to 6
- doc_starts: int32 [4096], P('seq'), may hold values 0 or 1
- norm_gain: float32 [1024], replicated, may hold values from 0.5 to 1.5
- gate_weight: float32 [1024, 2048], P('seq', 'mp'), may hold values from -0.1875 to 0.1875
- value_weight: float32 [1024, 2048], P('seq', 'mp'), may hold values from -0.1875 to 0.1875
- state_weight: float32 [1024, 288], P('seq'), may hold values from -0.1875 to 0.1875
- conv_value: float32 [5, 2048], replicated, may hold values from -0.5 to 0.5
- conv_state: float32 [5, 256], replicated, may hold values from -0.5 to 0.5
- head_params: float32 [3, 32], replicated, as said below
- gated_gain: float32 [2048], replicated, may hold values from 0.5 to 1.5
- out_weight: float32 [1024, 2048], P('seq', 'mp'), may hold values from -0.125 to 0.125
- norm_gain_velocity: float32 [1024], replicated, may hold values from -80 to 80
- gate_weight_velocity: float32 [1024, 2048], P('seq', 'mp'), may hold values from -80 to 80
- value_weight_velocity: float32 [1024, 2048], P('seq', 'mp'), may hold values from -80 to 80
- state_weight_velocity: float32 [1024, 288], P('seq'), may hold values from -80 to 80
- conv_value_velocity: float32 [5, 2048], replicated, may hold values from -80 to 80
- conv_state_velocity: float32 [5, 256], replicated, may hold values from -80 to 80
- head_params_velocity: float32 [3, 32], replicated, may hold values from -80 to 80
- gated_gain_velocity: float32 [2048], replicated, may hold values from -80 to 80
- out_weight_velocity: float32 [1024, 2048], P('seq', 'mp'), may hold values from -80 to 80
Outputs:
- layer_output: float32 [4096, 1024], P('seq')
- input_grad: float32 [4096, 1024], P('seq')
- norm_gain_grad: float32 [1024], replicated
- gate_weight_grad: float32 [1024, 2048], P('seq', 'mp')
- value_weight_grad: float32 [1024, 2048], P('seq', 'mp')
- state_weight_grad: float32 [1024, 288], P('seq')
- conv_value_grad: float32 [5, 2048], replicated
- conv_state_grad: float32 [5, 256], replicated
- head_params_grad: float32 [3, 32], replicated
- gated_gain_grad: float32 [2048], replicated
- out_weight_grad: float32 [1024, 2048], P('seq', 'mp')
- new_norm_gain: float32 [1024], replicated
- new_gate_weight: float32 [1024, 2048], P('seq', 'mp')
- new_value_weight: float32 [1024, 2048], P('seq', 'mp')
- new_state_weight: float32 [1024, 288], P('seq')
- new_conv_value: float32 [5, 2048], replicated
- new_conv_state: float32 [5, 256], replicated
- new_head_params: float32 [3, 32], replicated
- new_gated_gain: float32 [2048], replicated
- new_out_weight: float32 [1024, 2048], P('seq', 'mp')
- new_norm_gain_velocity: float32 [1024], replicated
- new_gate_weight_velocity: float32 [1024, 2048], P('seq', 'mp')
- new_value_weight_velocity: float32 [1024, 2048], P('seq', 'mp')
- new_state_weight_velocity: float32 [1024, 288], P('seq')
- new_conv_value_velocity: float32 [5, 2048], replicated
- new_conv_state_velocity: float32 [5, 256], replicated
- new_head_params_velocity: float32 [3, 32], replicated
- new_gated_gain_velocity: float32 [2048], replicated
- new_out_weight_velocity: float32 [1024, 2048], P('seq', 'mp')
The draws below stay inside these ranges and needn't reach their ends.
Inputs may be any that keep to these rules, and one draw needn't show every extreme that they name: `head_params`: row 0 holds step biases, row 1 logarithms of decay rates, row 2 skip coefficients.
All inputs are finite; a program needn't handle non-finite values. No bound on the sum of `doc_starts` on one device may be relied on, other than what follows from the above.
Results may differ from the reference program's by a relative error of at most 0.0003.
Values sent between devices are 32-bit elements; how exact they have to be, the bound alone decides.
No kernel may reach another device: no remote copies, remote signals or barrier semaphores. Data moves between devices by JAX's collectives and lax.ppermute only.
A program may use at most 256 MiB of HBM per device.

```python
import math
import jax
import jax.numpy as jnp
from jax import lax

D = 1024
DI = 2048
H = 32
P_SIZE = 64
N = 128
K = 4
GROUP = 256
TOK_DEV = 256
TOKENS = 4096


def draw_head_params(key, part):
    bias_key, rate_key, skip_key = jax.random.split(jax.random.fold_in(key, 7), 3)
    bias_row = jax.random.uniform(bias_key, (H,), jnp.float32, -4.6, -3.6)
    slowest = 2400.0 / (TOKENS * TOKENS)
    fastest = 1.5
    spread = jax.random.uniform(rate_key, (H,), jnp.float32, 0.0, 1.0)
    log_rate = jnp.log(slowest) + spread * (jnp.log(fastest) - jnp.log(slowest))
    skip_row = jax.random.uniform(skip_key, (H,), jnp.float32, 0.5, 1.5)
    return jnp.stack([bias_row, log_rate.astype(jnp.float32), skip_row])


def set_ends(entries, stream_key, smallest, largest):
    dims = entries.shape
    place = [jax.random.randint(jax.random.fold_in(stream_key, axis), (), 0, dims[axis]) for axis in range(len(dims))]
    entries = entries.at[tuple(place)].set(smallest)
    longest = dims.index(max(dims))
    place[longest] = (place[longest] + 1) % dims[longest]
    return entries.at[tuple(place)].set(largest)


def steps_of(rng, shape, cuts, smallest, top_value):
    def one(axis_at, parts):
        heights = jax.random.uniform(jax.random.fold_in(jax.random.fold_in(rng, 6), axis_at), (parts,), jnp.float32, smallest / len(cuts), top_value / len(cuts))
        return jnp.repeat(jnp.exp(heights), shape[axis_at] // parts).reshape((-1,) + (1,) * (len(shape) - axis_at - 1))

    factor_of = one(*cuts[0])
    for cut in cuts[1:]:
        factor_of = factor_of * one(*cut)
    return factor_of


def centred(stream_key, dims, scale, reach, cuts=(), held_as=jnp.bfloat16):
    values = jax.random.normal(stream_key, dims, jnp.float32) * scale
    if len(cuts) > 0:
        values = steps_of(stream_key, dims, cuts, -0.22, 0.18) * values
    return jnp.clip(values, min=-reach, max=reach).astype(held_as)


def setup_inputs(seed: int = 0) -> dict:
    seeds = jax.random.split(jax.random.key(seed), 22)
    return {
        "layer_input": centred(seeds[0], (TOKENS, D), 1.0, 6.0, ((0, 16),), jnp.float32),
        "cotangent": centred(seeds[1], (TOKENS, D), 1.0, 6.0, ((0, 16),), jnp.float32),
        "doc_starts": set_ends((jax.random.randint(seeds[2], (TOKENS,), 0, TOK_DEV * 16) < 1).astype(jnp.int32), jax.random.fold_in(seeds[2], 1), 0, 1),
        "norm_gain": jnp.clip(1.0 + 0.1 * jax.random.normal(seeds[3], (D,), jnp.float32), 0.5, 1.5),
        "gate_weight": centred(seeds[4], (D, DI), D ** -0.5, 0.1875, ((0, 16), (1, 2)), jnp.float32),
        "value_weight": centred(seeds[5], (D, DI), D ** -0.5, 0.1875, ((0, 16), (1, 2)), jnp.float32),
        "state_weight": centred(seeds[6], (D, 2 * N + H), D ** -0.5, 0.1875, ((0, 16),), jnp.float32),
        "conv_value": jnp.clip(jax.random.uniform(seeds[7], (K + 1, DI), jnp.float32, -0.5, 0.5), -0.5, 0.5),
        "conv_state": jnp.clip(jax.random.uniform(seeds[8], (K + 1, 2 * N), jnp.float32, -0.5, 0.5), -0.5, 0.5),
        "head_params": draw_head_params(jax.random.fold_in(seeds[21], 71), 0),
        "gated_gain": jnp.clip(1.0 + 0.1 * jax.random.normal(seeds[10], (DI,), jnp.float32), 0.5, 1.5),
        "out_weight": centred(seeds[11], (D, DI), DI ** -0.5, 0.125, ((0, 16), (1, 2)), jnp.float32),
        "norm_gain_velocity": centred(seeds[12], (D,), (0.2 * TOKENS ** 0.5), 80.0, (), jnp.float32),
        "gate_weight_velocity": centred(seeds[13], (D, DI), (0.2 * TOKENS ** 0.5), 80.0, ((0, 16), (1, 2)), jnp.float32),
        "value_weight_velocity": centred(seeds[14], (D, DI), (0.2 * TOKENS ** 0.5), 80.0, ((0, 16), (1, 2)), jnp.float32),
        "state_weight_velocity": centred(seeds[15], (D, 2 * N + H), (0.2 * TOKENS ** 0.5), 80.0, ((0, 16),), jnp.float32),
        "conv_value_velocity": centred(seeds[16], (K + 1, DI), (0.2 * TOKENS ** 0.5), 80.0, (), jnp.float32),
        "conv_state_velocity": centred(seeds[17], (K + 1, 2 * N), (0.2 * TOKENS ** 0.5), 80.0, (), jnp.float32),
        "head_params_velocity": centred(seeds[18], (3, H), (0.2 * TOKENS ** 0.5), 80.0, (), jnp.float32),
        "gated_gain_velocity": centred(seeds[19], (DI,), (0.2 * TOKENS ** 0.5), 80.0, (), jnp.float32),
        "out_weight_velocity": centred(seeds[20], (D, DI), (0.2 * TOKENS ** 0.5), 80.0, ((0, 16), (1, 2)), jnp.float32),
    }


highest = lax.Precision.HIGHEST
epsilon = 1e-05
momentum_decay = 0.95
matrix_rate = 0.03
vector_rate = 0.2
quintic_a = 3.4445
quintic_b = -4.775
quintic_c = 2.0315

def matmul(left, right):
    return jnp.dot(left, right, precision=highest)

def ssd_block(state, inputs):
    head_values, input_map, read_map, step_size, log_decay, starts = inputs
    length = head_values.shape[0]
    log_sums = jnp.cumsum(log_decay, 0)
    segment = jnp.cumsum(starts)
    position = jnp.arange(length)
    same = (position[:, None] >= position[None, :]) & (segment[:, None] == segment[None, :])
    causal_mask = same[:, :, None]
    log_gap = log_sums[:, None, :] - log_sums[None, :, :]
    decay_mat = jnp.where(causal_mask, jnp.exp(jnp.where(causal_mask, log_gap, 0.0)), 0.0)
    scores = matmul(read_map, input_map.T)
    scaled = head_values * step_size[:, :, None]
    intra = jnp.einsum('ijh,ij,jhp->ihp', decay_mat, scores, scaled, precision=highest)
    entry = jnp.exp(log_sums) * (segment == 0)[:, None]
    inter = entry[:, :, None] * jnp.einsum('hpn,in->ihp', state, read_map, precision=highest)
    tail = jnp.exp(log_sums[-1][None, :] - log_sums) * (segment == segment[-1])[:, None]
    decay = jnp.exp(log_sums[-1]) * (segment[-1] == 0)
    new_state = decay[:, None, None] * state + jnp.einsum('jh,jhp,jn->hpn', tail, scaled, input_map, precision=highest)
    return (new_state, intra + inter)

def block_forward(params, block_input, starts, carry):
    norm_gain, gate_weight, value_weight, state_weight, conv_value, conv_state, head_params, gated_gain, out_weight = params
    state, tail_rows, tail_starts = carry
    length = block_input.shape[0]
    normed = block_input * lax.rsqrt(lax.optimization_barrier(jnp.mean(block_input * block_input, 1, keepdims=True)) + epsilon)
    features = normed * norm_gain
    gate = matmul(features, gate_weight)
    value_raw = matmul(features, value_weight)
    state_raw = matmul(features, state_weight)
    mixed_in = jnp.concatenate([value_raw, state_raw[:, :2 * N]], 1)
    conv_all = jnp.concatenate([conv_value, conv_state], 1)
    padded = jnp.concatenate([tail_rows, mixed_in], 0)
    all_starts = jnp.concatenate([tail_starts, starts])
    cumulative = jnp.cumsum(all_starts)
    conv_pre = conv_all[K] + conv_all[0] * mixed_in
    for lag in range(1, K):
        keep = (cumulative[K - 1:] - cumulative[K - 1 - lag:K - 1 - lag + length] < 0.5).astype(jnp.float32)
        conv_pre = conv_pre + keep[:, None] * conv_all[lag] * padded[K - 1 - lag:K - 1 - lag + length]
    activated = jax.nn.silu(conv_pre)
    head_values = activated[:, :DI].reshape(length, H, P_SIZE)
    input_map = activated[:, DI:DI + N]
    read_map = activated[:, DI + N:]
    step_size = jax.nn.softplus(state_raw[:, 2 * N:] + head_params[0])
    log_decay = -jnp.exp(head_params[1]) * step_size
    span = math.gcd(length, GROUP)
    count = length // span
    pieces = (head_values.reshape(count, span, H, P_SIZE), input_map.reshape(count, span, N), read_map.reshape(count, span, N), step_size.reshape(count, span, H), log_decay.reshape(count, span, H), starts.reshape(count, span))
    new_state, ssd = lax.scan(ssd_block, state, pieces)
    ssd_out = (ssd.reshape(length, H, P_SIZE) + head_values * head_params[2][None, :, None]).reshape(length, DI)
    product = ssd_out * jax.nn.silu(gate)
    gated = product * lax.rsqrt(lax.optimization_barrier(jnp.mean(product * product, 1, keepdims=True)) + epsilon) * gated_gain
    output = block_input + lax.dot_general(gated, out_weight, (((1,), (1,)), ((), ())), precision=highest)
    return (output, (new_state, padded[length:], all_starts[length:]))

def orthogonal(block):
    current = block / (jnp.sqrt(jnp.sum(block * block)) + 1e-07)
    for sweep in range(5):
        gram = matmul(current.T, current)
        current = quintic_a * current + matmul(current, quintic_b * gram + quintic_c * matmul(gram, gram))
    return current

def head_blocks(update):
    blocks = update.reshape(D, H, P_SIZE).transpose(1, 0, 2)
    done = jax.vmap(orthogonal)(blocks)
    return done.transpose(1, 0, 2).reshape(D, DI)

def state_blocks(update):
    return jnp.concatenate([orthogonal(update[:, :N]), orthogonal(update[:, N:2 * N]), orthogonal(update[:, 2 * N:])], 1)

def muon_step(weight, gradient, velocity, blocks):
    new_velocity = momentum_decay * velocity + gradient
    update = gradient + momentum_decay * new_velocity
    return (weight - matrix_rate * 0.2 * math.sqrt(D) * blocks(update), new_velocity)

def vector_step(current, gradient, velocity):
    new_velocity = momentum_decay * velocity + gradient
    direction = gradient + momentum_decay * new_velocity
    magnitude = jnp.sqrt(jnp.mean(current * current))
    return (current - vector_rate * magnitude * direction / jnp.sqrt(jnp.mean(direction * direction) + 1e-06), new_velocity)

def reference(layer_input, cotangent, doc_starts, norm_gain, gate_weight, value_weight, state_weight, conv_value, conv_state, head_params, gated_gain, out_weight, norm_gain_velocity, gate_weight_velocity, value_weight_velocity, state_weight_velocity, conv_value_velocity, conv_state_velocity, head_params_velocity, gated_gain_velocity, out_weight_velocity):
    params = (norm_gain, gate_weight, value_weight, state_weight, conv_value, conv_state, head_params, gated_gain, out_weight)
    block = math.gcd(TOKENS, 4096)
    count = TOKENS // block
    inputs = layer_input.reshape(count, block, D)
    starts = doc_starts.astype(jnp.float32).reshape(count, block)
    cotangents = cotangent.reshape(count, block, D)
    start_carry = (jnp.zeros((H, P_SIZE, N), jnp.float32), jnp.zeros((K - 1, DI + 2 * N), jnp.float32), jnp.zeros((K - 1,), jnp.float32))

    def forward_step(carry, inputs_block):
        block_input, block_starts = inputs_block
        output, new_carry = block_forward(params, block_input, block_starts, carry)
        return (new_carry, (output, carry))
    _, (outputs, carries) = lax.scan(forward_step, start_carry, (inputs, starts))

    def backward_step(state, inputs_block):
        carry_grad, param_grads = state
        block_input, block_starts, block_cot, carry = inputs_block

        def local_block(param_set, block_in, carry_in):
            return block_forward(param_set, block_in, block_starts, carry_in)
        _, pullback = jax.vjp(local_block, params, block_input, carry)
        grads, block_input_grad, carry_in_grad = pullback((block_cot, carry_grad))
        return ((carry_in_grad, jax.tree.map(jnp.add, param_grads, grads)), block_input_grad)
    zero_grads = jax.tree.map(jnp.zeros_like, params)
    zero_carry = jax.tree.map(jnp.zeros_like, start_carry)
    (_, grads), input_grads = lax.scan(backward_step, (zero_carry, zero_grads), (inputs, starts, cotangents, carries), reverse=True)
    layer_output = outputs.reshape(TOKENS, D)
    input_grad = input_grads.reshape(TOKENS, D)
    norm_gain_grad, gate_weight_grad, value_weight_grad, state_weight_grad, conv_value_grad, conv_state_grad, head_params_grad, gated_gain_grad, out_weight_grad = grads
    new_gate_weight, new_gate_velocity = muon_step(gate_weight, gate_weight_grad, gate_weight_velocity, head_blocks)
    new_value_weight, new_value_velocity = muon_step(value_weight, value_weight_grad, value_weight_velocity, head_blocks)
    new_state_weight, new_state_velocity = muon_step(state_weight, state_weight_grad, state_weight_velocity, state_blocks)
    new_out_weight, new_out_velocity = muon_step(out_weight, out_weight_grad, out_weight_velocity, head_blocks)
    new_norm_gain, new_norm_velocity = vector_step(norm_gain, norm_gain_grad, norm_gain_velocity)
    new_conv_value, new_conv_value_velocity = vector_step(conv_value, conv_value_grad, conv_value_velocity)
    new_conv_state, new_conv_state_velocity = vector_step(conv_state, conv_state_grad, conv_state_velocity)
    new_head_params, new_head_velocity = vector_step(head_params, head_params_grad, head_params_velocity)
    new_gated_gain, new_gated_velocity = vector_step(gated_gain, gated_gain_grad, gated_gain_velocity)
    return (layer_output, input_grad, norm_gain_grad, gate_weight_grad, value_weight_grad, state_weight_grad, conv_value_grad, conv_state_grad, head_params_grad, gated_gain_grad, out_weight_grad, new_norm_gain, new_gate_weight, new_value_weight, new_state_weight, new_conv_value, new_conv_state, new_head_params, new_gated_gain, new_out_weight, new_norm_velocity, new_gate_velocity, new_value_velocity, new_state_velocity, new_conv_value_velocity, new_conv_state_velocity, new_head_velocity, new_gated_velocity, new_out_velocity)
```

```python
import functools

import jax
import jax.numpy as jnp
from jax import lax
from jax.experimental import pallas as pl
from jax.experimental.pallas import tpu as pltpu
from jax.sharding import PartitionSpec as P

D = 1024
DI = 2048
H = 32
P_SIZE = 64
N = 128
K = 4
LANES = 128


highest = lax.Precision.HIGHEST
high = lax.Precision.HIGH
epsilon = 1e-05
momentum_decay = 0.95
matrix_rate = 0.03
vector_rate = 0.2
quintic_a = 3.4445
quintic_b = -4.775
quintic_c = 2.0315


def passed_along(shard, axis, by):
    size = lax.axis_size(axis)
    pairs = [(i, i + by) for i in range(size) if 0 <= i + by < size]
    return lax.ppermute(shard, axis, pairs)


def swapped(shard):
    return lax.ppermute(shard, "mp", [(0, 1), (1, 0)])


def pair_sum(shard):
    return shard + swapped(shard)


def exchange(array):
    return lax.all_to_all(array, "seq", 0, 0, tiled=True)


def matmul(left, right):
    return jnp.dot(left, right, precision=high)


def dot_last(left, right):
    return lax.dot_general(left, right, (((1,), (1,)), ((), ())), precision=high)


def dot_first(left, right):
    return lax.dot_general(left, right, (((0,), (0,)), ((), ())), precision=high)


def silu_slope(value):
    sigma = jax.nn.sigmoid(value)
    return sigma * (1.0 + value * (1.0 - sigma))


def carry_kernel(reverse, part_ref, out_ref):
    count, rows, _ = out_ref.shape

    def one(lap, state):
        source = count - 1 - lap if reverse else lap
        out_ref[source] = state
        return part_ref[source, rows : rows + 1] * state + part_ref[source, :rows]

    lax.fori_loop(0, count, one, jnp.zeros((rows, N), jnp.float32))


def carried_in(decay, state, reverse):
    count = lax.axis_size("seq")
    heads = state.shape[0]
    rows = heads * P_SIZE // count
    owner = jnp.repeat(decay, P_SIZE).reshape(count, rows)[:, :1]
    part = jnp.concatenate(
        [state.reshape(count, rows, N), jnp.broadcast_to(owner[:, :, None], (count, 8, N))], 1
    )
    gathered = exchange(part)
    entering = pl.pallas_call(
        functools.partial(carry_kernel, reverse),
        out_shape=jax.ShapeDtypeStruct((count, rows, N), jnp.float32),
        name="carry",
    )(gathered)
    return exchange(entering).reshape(heads, P_SIZE, N)


def chain_kernel(gram_ref, out_ref):
    count, size, _ = gram_ref.shape
    row = lax.broadcasted_iota(jnp.int32, (size, size), 0)
    col = lax.broadcasted_iota(jnp.int32, (size, size), 1)
    eye = (row == col).astype(jnp.float32)
    grams = []
    totals = []
    for unit in range(count):
        gram = gram_ref[unit]
        norm = jnp.sqrt(jnp.sum(gram * eye, keepdims=True)) + 1e-07
        grams.append(gram / (norm * norm))
        totals.append(eye / norm)
    for sweep in range(5):
        squares = [jnp.dot(gram, gram, precision=highest) for gram in grams]
        steps = [
            quintic_a * eye + quintic_b * gram + quintic_c * square
            for gram, square in zip(grams, squares)
        ]
        totals = [
            jnp.dot(total, step, precision=highest) for total, step in zip(totals, steps)
        ]
        if sweep < 4:
            halves = [
                jnp.dot(step, gram, precision=highest) for step, gram in zip(steps, grams)
            ]
            grams = [
                jnp.dot(half, step, precision=highest) for half, step in zip(halves, steps)
            ]
    for unit in range(count):
        out_ref[unit] = totals[unit]


def chain(grams):
    return pl.pallas_call(
        chain_kernel,
        out_shape=jax.ShapeDtypeStruct(grams.shape, jnp.float32),
        name="chain",
    )(grams)


def padded_to(array, multiple):
    extra = -array.shape[0] % multiple
    return jnp.pad(array, ((0, extra),) + ((0, 0),) * (array.ndim - 1))


def head_grams(update):
    split = update.reshape(update.shape[0], -1, P_SIZE)
    return jnp.einsum("rup,ruq->upq", split, split, precision=highest)


def apply_heads(update, polynomials):
    split = update.reshape(update.shape[0], -1, P_SIZE)
    return jnp.einsum("rup,upq->ruq", split, polynomials, precision=highest).reshape(update.shape)


def vector_step(current, gradient, velocity):
    new_velocity = momentum_decay * velocity + gradient
    direction = gradient + momentum_decay * new_velocity
    magnitude = jnp.sqrt(jnp.mean(current * current))
    return (
        current
        - vector_rate * magnitude * direction / jnp.sqrt(jnp.mean(direction * direction) + 1e-06),
        new_velocity,
    )


def matrix_momentum(gradient, velocity):
    new_velocity = momentum_decay * velocity + gradient
    return new_velocity, gradient + momentum_decay * new_velocity


def body(
    layer_input,
    cotangent,
    doc_starts,
    norm_gain,
    gate_weight,
    value_weight,
    state_weight,
    conv_value,
    conv_state,
    head_params,
    gated_gain,
    out_weight,
    norm_gain_velocity,
    gate_weight_velocity,
    value_weight_velocity,
    state_weight_velocity,
    conv_value_velocity,
    conv_state_velocity,
    head_params_velocity,
    gated_gain_velocity,
    out_weight_velocity,
):
    seq_count = lax.axis_size("seq")
    model_count = lax.axis_size("mp")
    model_index = lax.axis_index("mp")
    rows = layer_input.shape[0]
    inner = DI // model_count
    heads = H // model_count
    inner_start = model_index * inner
    head_start = model_index * heads
    rim = K - 1
    mixed_full = lax.all_gather(
        jnp.concatenate([value_weight, state_weight], 1), "seq", axis=0, tiled=True
    )
    outer_full = lax.all_gather(
        jnp.concatenate([gate_weight, out_weight], 1), "seq", axis=0, tiled=True
    )
    gain_local = lax.dynamic_slice_in_dim(gated_gain, inner_start, inner, 0)
    conv_local = jnp.concatenate(
        [lax.dynamic_slice_in_dim(conv_value, inner_start, inner, 1), conv_state], 1
    )
    head_local = lax.dynamic_slice_in_dim(head_params, head_start, heads, 1)
    starts_float = doc_starts.astype(jnp.float32)
    scale = lax.rsqrt(jnp.mean(layer_input * layer_input, 1, keepdims=True) + epsilon)
    normed = layer_input * scale
    features = normed * norm_gain
    raw = matmul(features, mixed_full)
    mixed_in = raw[:, : inner + 2 * N]
    prev_starts = passed_along(starts_float[rows - rim :], "seq", 1)
    prev_rows = passed_along(mixed_in[rows - rim :], "seq", 1)
    padded = jnp.concatenate([prev_rows, mixed_in], 0)
    cumulative = jnp.cumsum(jnp.concatenate([prev_starts, starts_float]))
    keeps = [jnp.ones((rows,), jnp.float32)]
    for lag in range(1, K):
        keeps.append(
            (cumulative[rim:] - cumulative[rim - lag : rim - lag + rows] < 0.5).astype(jnp.float32)
        )
    conv_pre = conv_local[K] + jnp.zeros_like(mixed_in)
    for lag in range(K):
        conv_pre = (
            conv_pre + keeps[lag][:, None] * conv_local[lag] * padded[rim - lag : rim - lag + rows]
        )
    activated = jax.nn.silu(conv_pre)
    head_values = activated[:, :inner].reshape(rows, heads, P_SIZE)
    input_map = activated[:, inner : inner + N]
    read_map = activated[:, inner + N :]
    step_pre = (
        lax.dynamic_slice_in_dim(raw, inner + 2 * N + head_start, heads, 1) + head_local[0]
    )
    step_size = jax.nn.softplus(step_pre)
    rate = -jnp.exp(head_local[1])
    skip = head_local[2]
    log_sums = jnp.cumsum(step_size * rate, 0)
    segment = jnp.cumsum(starts_float)
    position = jnp.arange(rows)
    causal_mask = (
        (position[:, None] >= position[None, :]) & (segment[:, None] == segment[None, :])
    )[None]
    head_logs = log_sums.T
    log_gap = head_logs[:, :, None] - head_logs[:, None, :]
    decay_mat = jnp.where(causal_mask, jnp.exp(jnp.where(causal_mask, log_gap, 0.0)), 0.0)
    scores = dot_last(read_map, input_map)
    weighted = decay_mat * scores[None]
    scaled = head_values * step_size[..., None]
    last_log = log_sums[-1]
    last_segment = segment[-1]
    tail_weight = jnp.exp(last_log[None] - log_sums) * (segment == last_segment)[:, None]
    tail_scaled = scaled * tail_weight[..., None]
    block_state = jnp.einsum("jhp,jn->hpn", tail_scaled, input_map, precision=high)
    block_decay = jnp.exp(last_log) * (last_segment == 0)
    entry_weight = jnp.exp(log_sums) * (segment == 0)[:, None]
    entries = carried_in(block_decay, block_state, False)
    intra = jnp.einsum("hij,jhp->ihp", weighted, scaled, precision=high)
    state_read = jnp.einsum("hpn,in->ihp", entries, read_map, precision=high)
    ssd_out = (
        intra + entry_weight[..., None] * state_read + head_values * skip[None, :, None]
    ).reshape(rows, inner)
    gate_full = outer_full[:, :inner]
    out_full = outer_full[:, inner:]
    gate = matmul(features, gate_full)
    grad_gated = matmul(cotangent, out_full)
    grad_hat = grad_gated * gain_local
    gate_act = jax.nn.silu(gate)
    product = ssd_out * gate_act
    row_sums = pair_sum(jnp.stack([jnp.sum(product * product, 1), jnp.sum(product * grad_hat, 1)]))
    gate_scale = lax.rsqrt(row_sums[0] / DI + epsilon)[:, None]
    inner_sum = row_sums[1][:, None]
    gated = product * gate_scale * gain_local
    grad_product = gate_scale * (grad_hat - product * gate_scale * gate_scale * (inner_sum / DI))
    grad_gate = grad_product * ssd_out * silu_slope(gate)
    outer_reduced = lax.psum_scatter(
        jnp.concatenate([dot_first(features, grad_gate), dot_first(cotangent, gated)], 1),
        "seq",
        scatter_dimension=0,
        tiled=True,
    )
    layer_output = layer_input + pair_sum(dot_last(gated, out_full))
    gated_gain_part = jnp.sum(grad_gated * product * gate_scale, 0)
    ssd_grad = (grad_product * gate_act).reshape(rows, heads, P_SIZE)
    skip_grad = jnp.sum(ssd_grad * head_values, (0, 2))
    weighted_grad = ssd_grad * entry_weight[..., None]
    enter_grad = jnp.einsum("ihp,in->hpn", weighted_grad, read_map, precision=high)
    out_grads = carried_in(block_decay, enter_grad, True)
    read_grad = jnp.einsum("ihp,hpn->in", weighted_grad, entries, precision=high)
    logs_grad = jnp.sum(ssd_grad * state_read, 2) * entry_weight
    mix_grad = jnp.einsum("ihp,jhp->hij", ssd_grad, scaled, precision=high)
    scaled_grad = jnp.einsum("hij,ihp->jhp", weighted, ssd_grad, precision=high)
    score_grad = jnp.sum(mix_grad * decay_mat, 0)
    read_grad = read_grad + matmul(score_grad, input_map)
    input_grad_map = dot_first(score_grad, read_map)
    decay_term = mix_grad * weighted
    logs_grad = logs_grad + (jnp.sum(decay_term, 2) - jnp.sum(decay_term, 1)).T
    from_state = jnp.einsum("hpn,jn->jhp", out_grads, input_map, precision=high)
    scaled_grad = scaled_grad + tail_weight[..., None] * from_state
    input_grad_map = input_grad_map + jnp.einsum(
        "hpn,jhp->jn", out_grads, tail_scaled, precision=high
    )
    tail_grad = jnp.sum(from_state * tail_scaled, 2)
    last_grad = jnp.sum(tail_grad, 0) + jnp.sum(out_grads * entries, (1, 2)) * block_decay
    logs_grad = logs_grad - tail_grad
    decay_log_grad = jnp.flip(jnp.cumsum(jnp.flip(logs_grad, 0), 0), 0) + last_grad[None]
    grad_values = ssd_grad * skip[None, :, None] + scaled_grad * step_size[..., None]
    step_grad = jnp.sum(scaled_grad * head_values, 2) + decay_log_grad * rate
    rate_grad = jnp.sum(decay_log_grad * step_size, 0)
    log_rate_grad = rate_grad * rate
    step_pre_grad = step_grad * jax.nn.sigmoid(step_pre)
    bias_grad = jnp.sum(step_pre_grad, 0)
    step_full = lax.dynamic_update_slice_in_dim(
        jnp.zeros((rows, H), jnp.float32), step_pre_grad, head_start, 1
    )
    shared = pair_sum(jnp.concatenate([input_grad_map, read_grad, step_full], 1))
    act_grad = jnp.concatenate([grad_values.reshape(rows, inner), shared[:, : 2 * N]], 1)
    pre_grad = act_grad * silu_slope(conv_pre)
    conv_rows = []
    padded_grad = jnp.zeros_like(padded)
    for lag in range(K):
        masked = keeps[lag][:, None] * pre_grad
        conv_rows.append(jnp.sum(masked * padded[rim - lag : rim - lag + rows], 0))
        padded_grad = padded_grad + jnp.pad(masked * conv_local[lag], ((rim - lag, lag), (0, 0)))
    conv_rows.append(jnp.sum(pre_grad, 0))
    conv_local_grad = jnp.stack(conv_rows)
    spill = passed_along(padded_grad[:rim], "seq", -1)
    mixed_grad = padded_grad[rim:] + jnp.pad(spill, ((rows - rim, 0), (0, 0)))
    raw_grad = jnp.concatenate([mixed_grad, shared[:, 2 * N :]], 1)
    mixed_reduced = lax.psum_scatter(
        dot_first(features, raw_grad), "seq", scatter_dimension=0, tiled=True
    )
    once = jnp.where(jnp.arange(raw_grad.shape[1]) < inner, 1.0, 1.0 / model_count)
    features_grad = pair_sum(
        dot_last(grad_gate, gate_full) + dot_last(raw_grad * once, mixed_full)
    )
    norm_gain_part = jnp.sum(features_grad * normed, 0)
    gain_grad_in = features_grad * norm_gain
    input_grad = cotangent + scale * (
        gain_grad_in - normed * jnp.mean(gain_grad_in * normed, 1, keepdims=True)
    )

    factor = matrix_rate * 0.2 * D**0.5
    gate_weight_grad = outer_reduced[:, :inner]
    out_weight_grad = outer_reduced[:, inner:]
    new_gate_velocity, gate_update = matrix_momentum(gate_weight_grad, gate_weight_velocity)
    new_out_velocity, out_update = matrix_momentum(out_weight_grad, out_weight_velocity)
    outer_update = jnp.concatenate([gate_update, out_update], 1)
    outer_grams = padded_to(head_grams(outer_update), seq_count)
    per = outer_grams.shape[0] // seq_count
    outer_own = jnp.sum(exchange(outer_grams).reshape(seq_count, per, P_SIZE, P_SIZE), 0)
    outer_own = chain(outer_own)
    outer_poly = exchange(
        jnp.broadcast_to(outer_own[None], (seq_count,) + outer_own.shape).reshape(
            outer_grams.shape
        )
    )[: 2 * heads]
    outer_orth = apply_heads(outer_update, outer_poly)
    new_gate_weight = gate_weight - factor * outer_orth[:, :inner]
    new_out_weight = out_weight - factor * outer_orth[:, inner:]

    value_weight_grad = mixed_reduced[:, :inner]
    state_weight_grad = mixed_reduced[:, inner:]
    new_value_velocity, value_update = matrix_momentum(value_weight_grad, value_weight_velocity)
    new_state_velocity, state_update = matrix_momentum(state_weight_grad, state_weight_velocity)
    value_grams = padded_to(head_grams(value_update), seq_count)
    per = value_grams.shape[0] // seq_count
    value_rows = per * P_SIZE * P_SIZE // LANES
    map_update = state_update[:, : 2 * N].reshape(-1, 2, N)
    step_update = state_update[:, 2 * N :]
    map_grams = jnp.einsum("rup,ruq->upq", map_update, map_update, precision=highest)
    step_gram = lax.dot_general(
        step_update, step_update, (((0,), (0,)), ((), ())), precision=highest
    )
    small = jnp.concatenate(
        [
            map_grams.reshape(2 * N, N),
            jnp.pad(step_gram, ((0, 0), (0, N - H))),
            norm_gain_part.reshape(-1, LANES),
            conv_local_grad.reshape(-1, LANES),
            gated_gain_part.reshape(-1, LANES),
            jnp.pad(jnp.stack([bias_grad, log_rate_grad, skip_grad]), ((0, 0), (0, LANES - heads))),
        ],
        0,
    )
    small = padded_to(small, 8 * seq_count)
    small_rows = small.shape[0] // seq_count
    summed = jnp.sum(
        exchange(
            jnp.concatenate(
                [
                    value_grams.reshape(seq_count, value_rows, LANES),
                    small.reshape(seq_count, small_rows, LANES),
                ],
                1,
            )
        ),
        0,
    )
    value_own = chain(summed[:value_rows].reshape(per, P_SIZE, P_SIZE))
    told = jnp.concatenate([value_own.reshape(value_rows, LANES), summed[value_rows:]], 0)
    told = exchange(jnp.broadcast_to(told[None], (seq_count,) + told.shape))
    value_poly = told[:, :value_rows].reshape(seq_count * per, P_SIZE, P_SIZE)[:heads]
    small = told[:, value_rows:].reshape(seq_count * small_rows, LANES)
    state_poly = chain(
        jnp.stack(
            [small[:N], small[N : 2 * N], jnp.pad(small[2 * N : 2 * N + H], ((0, N - H), (0, 0)))]
        )
    )
    value_orth = apply_heads(value_update, value_poly)
    state_orth = jnp.concatenate(
        [
            jnp.einsum("rup,upq->ruq", map_update, state_poly[:2], precision=highest).reshape(
                -1, 2 * N
            ),
            jnp.dot(step_update, state_poly[2, :H, :H], precision=highest),
        ],
        1,
    )
    new_value_weight = value_weight - factor * value_orth
    new_state_weight = state_weight - factor * state_orth

    vectors = small[2 * N + H :]
    at = D // LANES
    norm_gain_grad = vectors[:at].reshape(D)
    other = swapped(vectors)
    first = jnp.where(model_index == 0, vectors, other)
    second = jnp.where(model_index == 0, other, vectors)
    conv_rows = (K + 1) * (inner + 2 * N) // LANES
    conv_first, conv_second = (
        side[at : at + conv_rows].reshape(K + 1, inner + 2 * N) for side in (first, second)
    )
    conv_value_grad = jnp.concatenate([conv_first[:, :inner], conv_second[:, :inner]], 1)
    conv_state_grad = conv_first[:, inner:]
    at = at + conv_rows
    gated_rows = inner // LANES
    gated_gain_grad = jnp.concatenate(
        [first[at : at + gated_rows].reshape(inner), second[at : at + gated_rows].reshape(inner)]
    )
    at = at + gated_rows
    head_params_grad = jnp.concatenate(
        [first[at : at + 3, :heads], second[at : at + 3, :heads]], 1
    )
    new_norm_gain, new_norm_velocity = vector_step(norm_gain, norm_gain_grad, norm_gain_velocity)
    new_conv_value, new_conv_value_velocity = vector_step(
        conv_value, conv_value_grad, conv_value_velocity
    )
    new_conv_state, new_conv_state_velocity = vector_step(
        conv_state, conv_state_grad, conv_state_velocity
    )
    new_head_params, new_head_velocity = vector_step(
        head_params, head_params_grad, head_params_velocity
    )
    new_gated_gain, new_gated_velocity = vector_step(
        gated_gain, gated_gain_grad, gated_gain_velocity
    )
    return (
        layer_output,
        input_grad,
        norm_gain_grad,
        gate_weight_grad,
        value_weight_grad,
        state_weight_grad,
        conv_value_grad,
        conv_state_grad,
        head_params_grad,
        gated_gain_grad,
        out_weight_grad,
        new_norm_gain,
        new_gate_weight,
        new_value_weight,
        new_state_weight,
        new_conv_value,
        new_conv_state,
        new_head_params,
        new_gated_gain,
        new_out_weight,
        new_norm_velocity,
        new_gate_velocity,
        new_value_velocity,
        new_state_velocity,
        new_conv_value_velocity,
        new_conv_state_velocity,
        new_head_velocity,
        new_gated_velocity,
        new_out_velocity,
    )


def solution(mesh):
    return jax.shard_map(
        body,
        mesh=mesh,
        in_specs=(
            P("seq", None),
            P("seq", None),
            P("seq"),
            P(),
            P("seq", "mp"),
            P("seq", "mp"),
            P("seq", None),
            P(),
            P(),
            P(),
            P(),
            P("seq", "mp"),
            P(),
            P("seq", "mp"),
            P("seq", "mp"),
            P("seq", None),
            P(),
            P(),
            P(),
            P(),
            P("seq", "mp"),
        ),
        out_specs=(
            P("seq", None),
            P("seq", None),
            P(),
            P("seq", "mp"),
            P("seq", "mp"),
            P("seq", None),
            P(),
            P(),
            P(),
            P(),
            P("seq", "mp"),
            P(),
            P("seq", "mp"),
            P("seq", "mp"),
            P("seq", None),
            P(),
            P(),
            P(),
            P(),
            P("seq", "mp"),
            P(),
            P("seq", "mp"),
            P("seq", "mp"),
            P("seq", None),
            P(),
            P(),
            P(),
            P(),
            P("seq", "mp"),
        ),
        check_vma=False,
    )
```

```python
import functools

import jax
import jax.numpy as jnp
from jax import lax
from jax.experimental import pallas as pl
from jax.experimental.pallas import tpu as pltpu
from jax.sharding import PartitionSpec as P

D = 1024
DI = 2048
H = 32
P_SIZE = 64
N = 128
K = 4
LANES = 128


highest = lax.Precision.HIGHEST
high = lax.Precision.HIGH
epsilon = 1e-05
momentum_decay = 0.95
matrix_rate = 0.03
vector_rate = 0.2
quintic_a = 3.4445
quintic_b = -4.775
quintic_c = 2.0315


def passed_along(shard, axis, by):
    size = lax.axis_size(axis)
    pairs = [(i, i + by) for i in range(size) if 0 <= i + by < size]
    return lax.ppermute(shard, axis, pairs)


def swapped(shard):
    return lax.ppermute(shard, "mp", [(0, 1), (1, 0)])


def pair_sum(shard):
    return shard + swapped(shard)


def exchange(array):
    return lax.all_to_all(array, "seq", 0, 0, tiled=True)


def matmul(left, right):
    return jnp.dot(left, right, precision=high)


def dot_last(left, right):
    return lax.dot_general(left, right, (((1,), (1,)), ((), ())), precision=high)


def dot_first(left, right):
    return lax.dot_general(left, right, (((0,), (0,)), ((), ())), precision=high)


def silu_slope(value):
    sigma = jax.nn.sigmoid(value)
    return sigma * (1.0 + value * (1.0 - sigma))


def carry_kernel(reverse, part_ref, out_ref):
    count, rows, _ = out_ref.shape

    def one(lap, state):
        source = count - 1 - lap if reverse else lap
        out_ref[source] = state
        return part_ref[source, rows : rows + 1] * state + part_ref[source, :rows]

    lax.fori_loop(0, count, one, jnp.zeros((rows, N), jnp.float32))


def carried_in(decay, state, reverse):
    count = lax.axis_size("seq")
    heads = state.shape[0]
    rows = heads * P_SIZE // count
    owner = jnp.repeat(decay, P_SIZE).reshape(count, rows)[:, :1]
    part = jnp.concatenate(
        [state.reshape(count, rows, N), jnp.broadcast_to(owner[:, :, None], (count, 8, N))], 1
    )
    gathered = exchange(part)
    entering = pl.pallas_call(
        functools.partial(carry_kernel, reverse),
        out_shape=jax.ShapeDtypeStruct((count, rows, N), jnp.float32),
        name="carry",
    )(gathered)
    return exchange(entering).reshape(heads, P_SIZE, N)


def chain_kernel(gram_ref, out_ref):
    count, size, _ = gram_ref.shape
    row = lax.broadcasted_iota(jnp.int32, (size, size), 0)
    col = lax.broadcasted_iota(jnp.int32, (size, size), 1)
    eye = (row == col).astype(jnp.float32)
    grams = []
    totals = []
    for unit in range(count):
        gram = gram_ref[unit]
        norm = jnp.sqrt(jnp.sum(gram * eye, keepdims=True)) + 1e-07
        grams.append(gram / (norm * norm))
        totals.append(eye / norm)
    for sweep in range(5):
        squares = [jnp.dot(gram, gram, precision=highest) for gram in grams]
        steps = [
            quintic_a * eye + quintic_b * gram + quintic_c * square
            for gram, square in zip(grams, squares)
        ]
        totals = [
            jnp.dot(total, step, precision=highest) for total, step in zip(totals, steps)
        ]
        if sweep < 4:
            halves = [
                jnp.dot(step, gram, precision=highest) for step, gram in zip(steps, grams)
            ]
            grams = [
                jnp.dot(half, step, precision=highest) for half, step in zip(halves, steps)
            ]
    for unit in range(count):
        out_ref[unit] = totals[unit]


def chain(grams):
    return pl.pallas_call(
        chain_kernel,
        out_shape=jax.ShapeDtypeStruct(grams.shape, jnp.float32),
        name="chain",
    )(grams)


def padded_to(array, multiple):
    extra = -array.shape[0] % multiple
    return jnp.pad(array, ((0, extra),) + ((0, 0),) * (array.ndim - 1))


def scatter_ready(parts):
    width = sum(part.shape[1] for part in parts)
    extra = -width % 96
    if extra:
        parts = parts + [jnp.zeros((parts[0].shape[0], extra), jnp.float32)]
    return jnp.concatenate(parts, 1)


def head_grams(update):
    split = update.reshape(update.shape[0], -1, P_SIZE)
    return jnp.einsum("rup,ruq->upq", split, split, precision=highest)


def apply_heads(update, polynomials):
    split = update.reshape(update.shape[0], -1, P_SIZE)
    return jnp.einsum("rup,upq->ruq", split, polynomials, precision=highest).reshape(update.shape)


def gathered_sum(grams, others):
    count = lax.axis_size("seq")
    others = padded_to(others, 8 * count)
    own_rows = others.shape[0] // count
    sent = jnp.concatenate(
        [grams.reshape(count, -1, LANES), others.reshape(count, own_rows, LANES)], 1
    )
    return jnp.sum(exchange(sent), 0), own_rows


def told_all(own, others, gram_rows, other_rows):
    count = lax.axis_size("seq")
    told = jnp.concatenate([own.reshape(gram_rows, LANES), others], 0)
    told = exchange(jnp.broadcast_to(told[None], (count,) + told.shape))
    return (
        told[:, :gram_rows].reshape(-1, P_SIZE, P_SIZE),
        told[:, gram_rows:].reshape(count * other_rows, LANES),
    )


def vector_step(current, gradient, velocity):
    new_velocity = momentum_decay * velocity + gradient
    direction = gradient + momentum_decay * new_velocity
    magnitude = jnp.sqrt(jnp.mean(current * current))
    return (
        current
        - vector_rate * magnitude * direction / jnp.sqrt(jnp.mean(direction * direction) + 1e-06),
        new_velocity,
    )


def matrix_momentum(gradient, velocity):
    new_velocity = momentum_decay * velocity + gradient
    return new_velocity, gradient + momentum_decay * new_velocity


def body(
    layer_input,
    cotangent,
    doc_starts,
    norm_gain,
    gate_weight,
    value_weight,
    state_weight,
    conv_value,
    conv_state,
    head_params,
    gated_gain,
    out_weight,
    norm_gain_velocity,
    gate_weight_velocity,
    value_weight_velocity,
    state_weight_velocity,
    conv_value_velocity,
    conv_state_velocity,
    head_params_velocity,
    gated_gain_velocity,
    out_weight_velocity,
):
    seq_count = lax.axis_size("seq")
    model_count = lax.axis_size("mp")
    model_index = lax.axis_index("mp")
    rows = layer_input.shape[0]
    inner = DI // model_count
    heads = H // model_count
    inner_start = model_index * inner
    head_start = model_index * heads
    rim = K - 1
    own_columns = inner + N + heads
    own_map = lax.dynamic_slice_in_dim(state_weight, model_index * N, N, 1)
    own_step = lax.dynamic_slice_in_dim(state_weight, 2 * N + head_start, heads, 1)
    mixed_full = lax.all_gather(
        jnp.concatenate([value_weight, own_map, own_step], 1), "seq", axis=0, tiled=True
    )
    outer_full = lax.all_gather(
        jnp.concatenate([gate_weight, out_weight], 1), "seq", axis=0, tiled=True
    )
    gain_local = lax.dynamic_slice_in_dim(gated_gain, inner_start, inner, 0)
    conv_local = jnp.concatenate(
        [
            lax.dynamic_slice_in_dim(conv_value, inner_start, inner, 1),
            lax.dynamic_slice_in_dim(conv_state, model_index * N, N, 1),
        ],
        1,
    )
    head_local = lax.dynamic_slice_in_dim(head_params, head_start, heads, 1)
    starts_float = doc_starts.astype(jnp.float32)
    scale = lax.rsqrt(jnp.mean(layer_input * layer_input, 1, keepdims=True) + epsilon)
    normed = layer_input * scale
    features = normed * norm_gain
    raw = jnp.dot(features, mixed_full, precision=highest)
    mixed_in = raw[:, : inner + N]
    prev_starts = passed_along(starts_float[rows - rim :], "seq", 1)
    prev_rows = passed_along(mixed_in[rows - rim :], "seq", 1)
    padded = jnp.concatenate([prev_rows, mixed_in], 0)
    cumulative = jnp.cumsum(jnp.concatenate([prev_starts, starts_float]))
    keeps = [jnp.ones((rows,), jnp.float32)]
    for lag in range(1, K):
        keeps.append(
            (cumulative[rim:] - cumulative[rim - lag : rim - lag + rows] < 0.5).astype(jnp.float32)
        )
    conv_pre = conv_local[K] + jnp.zeros_like(mixed_in)
    for lag in range(K):
        conv_pre = (
            conv_pre + keeps[lag][:, None] * conv_local[lag] * padded[rim - lag : rim - lag + rows]
        )
    activated = jax.nn.silu(conv_pre)
    head_values = activated[:, :inner].reshape(rows, heads, P_SIZE)
    this_map = activated[:, inner:]
    other_map = swapped(this_map)
    input_map = jnp.where(model_index == 0, this_map, other_map)
    read_map = jnp.where(model_index == 0, other_map, this_map)
    step_pre = raw[:, inner + N :] + head_local[0]
    step_size = jax.nn.softplus(step_pre)
    rate = -jnp.exp(head_local[1])
    skip = head_local[2]
    log_sums = jnp.cumsum(step_size * rate, 0)
    segment = jnp.cumsum(starts_float)
    position = jnp.arange(rows)
    causal_mask = (
        (position[:, None] >= position[None, :]) & (segment[:, None] == segment[None, :])
    )[None]
    head_logs = log_sums.T
    log_gap = head_logs[:, :, None] - head_logs[:, None, :]
    decay_mat = jnp.where(causal_mask, jnp.exp(jnp.where(causal_mask, log_gap, 0.0)), 0.0)
    scores = lax.dot_general(read_map, input_map, (((1,), (1,)), ((), ())), precision=highest)
    weighted = decay_mat * scores[None]
    scaled = head_values * step_size[..., None]
    last_log = log_sums[-1]
    last_segment = segment[-1]
    tail_weight = jnp.exp(last_log[None] - log_sums) * (segment == last_segment)[:, None]
    tail_scaled = scaled * tail_weight[..., None]
    block_state = jnp.einsum("jhp,jn->hpn", tail_scaled, input_map, precision=highest)
    block_decay = jnp.exp(last_log) * (last_segment == 0)
    entry_weight = jnp.exp(log_sums) * (segment == 0)[:, None]
    entries = carried_in(block_decay, block_state, False)
    intra = jnp.einsum("hij,jhp->ihp", weighted, scaled, precision=highest)
    state_read = jnp.einsum("hpn,in->ihp", entries, read_map, precision=highest)
    ssd_out = (
        intra + entry_weight[..., None] * state_read + head_values * skip[None, :, None]
    ).reshape(rows, inner)
    gate_full = outer_full[:, :inner]
    out_full = outer_full[:, inner:]
    gate = matmul(features, gate_full)
    grad_gated = matmul(cotangent, out_full)
    grad_hat = grad_gated * gain_local
    gate_act = jax.nn.silu(gate)
    product = ssd_out * gate_act
    row_sums = pair_sum(jnp.stack([jnp.sum(product * product, 1), jnp.sum(product * grad_hat, 1)]))
    gate_scale = lax.rsqrt(row_sums[0] / DI + epsilon)[:, None]
    inner_sum = row_sums[1][:, None]
    gated = product * gate_scale * gain_local
    grad_product = gate_scale * (grad_hat - product * gate_scale * gate_scale * (inner_sum / DI))
    grad_gate = grad_product * ssd_out * silu_slope(gate)
    outer_partial = scatter_ready([dot_first(features, grad_gate), dot_first(cotangent, gated)])
    outer_partial, grad_product = lax.optimization_barrier((outer_partial, grad_product))
    outer_reduced = lax.psum_scatter(outer_partial, "seq", scatter_dimension=0, tiled=True)
    layer_output = layer_input + pair_sum(dot_last(gated, out_full))
    gated_gain_part = jnp.sum(grad_gated * product * gate_scale, 0)
    ssd_grad = (grad_product * gate_act).reshape(rows, heads, P_SIZE)
    skip_grad = jnp.sum(ssd_grad * head_values, (0, 2))
    weighted_grad = ssd_grad * entry_weight[..., None]
    enter_grad = jnp.einsum("ihp,in->hpn", weighted_grad, read_map, precision=highest)
    out_grads = carried_in(block_decay, enter_grad, True)
    read_grad = jnp.einsum("ihp,hpn->in", weighted_grad, entries, precision=highest)
    logs_grad = jnp.sum(ssd_grad * state_read, 2) * entry_weight
    mix_grad = jnp.einsum("ihp,jhp->hij", ssd_grad, scaled, precision=highest)
    scaled_grad = jnp.einsum("hij,ihp->jhp", weighted, ssd_grad, precision=highest)
    score_grad = jnp.sum(mix_grad * decay_mat, 0)
    read_grad = read_grad + jnp.dot(score_grad, input_map, precision=highest)
    input_grad_map = lax.dot_general(
        score_grad, read_map, (((0,), (0,)), ((), ())), precision=highest
    )
    decay_term = mix_grad * weighted
    logs_grad = logs_grad + (jnp.sum(decay_term, 2) - jnp.sum(decay_term, 1)).T
    from_state = jnp.einsum("hpn,jn->jhp", out_grads, input_map, precision=highest)
    scaled_grad = scaled_grad + tail_weight[..., None] * from_state
    input_grad_map = input_grad_map + jnp.einsum(
        "hpn,jhp->jn", out_grads, tail_scaled, precision=highest
    )
    tail_grad = jnp.sum(from_state * tail_scaled, 2)
    last_grad = jnp.sum(tail_grad, 0) + jnp.sum(out_grads * entries, (1, 2)) * block_decay
    logs_grad = logs_grad - tail_grad
    decay_log_grad = jnp.flip(jnp.cumsum(jnp.flip(logs_grad, 0), 0), 0) + last_grad[None]
    grad_values = ssd_grad * skip[None, :, None] + scaled_grad * step_size[..., None]
    step_grad = jnp.sum(scaled_grad * head_values, 2) + decay_log_grad * rate
    rate_grad = jnp.sum(decay_log_grad * step_size, 0)
    log_rate_grad = rate_grad * rate
    step_pre_grad = step_grad * jax.nn.sigmoid(step_pre)
    bias_grad = jnp.sum(step_pre_grad, 0)
    this_grad = jnp.where(model_index == 0, input_grad_map, read_grad)
    other_grad = jnp.where(model_index == 0, read_grad, input_grad_map)
    act_grad = jnp.concatenate(
        [grad_values.reshape(rows, inner), this_grad + swapped(other_grad)], 1
    )
    pre_grad = act_grad * silu_slope(conv_pre)
    conv_rows = []
    padded_grad = jnp.zeros_like(padded)
    for lag in range(K):
        masked = keeps[lag][:, None] * pre_grad
        conv_rows.append(jnp.sum(masked * padded[rim - lag : rim - lag + rows], 0))
        padded_grad = padded_grad + jnp.pad(masked * conv_local[lag], ((rim - lag, lag), (0, 0)))
    conv_rows.append(jnp.sum(pre_grad, 0))
    conv_local_grad = jnp.stack(conv_rows)
    spill = passed_along(padded_grad[:rim], "seq", -1)
    mixed_grad = padded_grad[rim:] + jnp.pad(spill, ((rows - rim, 0), (0, 0)))
    raw_grad = jnp.concatenate([mixed_grad, step_pre_grad], 1)
    mixed_partial = scatter_ready([dot_first(features, raw_grad)])
    mixed_partial, raw_grad = lax.optimization_barrier((mixed_partial, raw_grad))
    mixed_reduced = lax.psum_scatter(mixed_partial, "seq", scatter_dimension=0, tiled=True)
    features_grad = pair_sum(dot_last(grad_gate, gate_full) + dot_last(raw_grad, mixed_full))
    norm_gain_part = jnp.sum(features_grad * normed, 0)
    gain_grad_in = features_grad * norm_gain
    input_grad = cotangent + scale * (
        gain_grad_in - normed * jnp.mean(gain_grad_in * normed, 1, keepdims=True)
    )

    factor = matrix_rate * 0.2 * D**0.5
    gate_weight_grad = outer_reduced[:, :inner]
    out_weight_grad = outer_reduced[:, inner : 2 * inner]
    new_gate_velocity, gate_update = matrix_momentum(gate_weight_grad, gate_weight_velocity)
    new_out_velocity, out_update = matrix_momentum(out_weight_grad, out_weight_velocity)
    outer_update = jnp.concatenate([gate_update, out_update], 1)
    outer_grams = padded_to(head_grams(outer_update), seq_count)
    per = outer_grams.shape[0] // seq_count
    outer_rows = per * P_SIZE * P_SIZE // LANES
    vectors = jnp.concatenate(
        [
            norm_gain_part.reshape(-1, LANES),
            conv_local_grad.reshape(-1, LANES),
            gated_gain_part.reshape(-1, LANES),
            jnp.pad(jnp.stack([bias_grad, log_rate_grad, skip_grad]), ((0, 0), (0, LANES - heads))),
        ],
        0,
    )
    summed, vector_rows = gathered_sum(outer_grams, vectors)
    outer_own = chain(summed[:outer_rows].reshape(per, P_SIZE, P_SIZE))
    outer_poly, vectors = told_all(outer_own, summed[outer_rows:], outer_rows, vector_rows)
    outer_orth = apply_heads(outer_update, outer_poly[: 2 * heads])
    new_gate_weight = gate_weight - factor * outer_orth[:, :inner]
    new_out_weight = out_weight - factor * outer_orth[:, inner:]

    at = D // LANES
    norm_gain_grad = vectors[:at].reshape(D)
    other = swapped(vectors)
    first = jnp.where(model_index == 0, vectors, other)
    second = jnp.where(model_index == 0, other, vectors)
    conv_rows = (K + 1) * (inner + N) // LANES
    conv_first, conv_second = (
        side[at : at + conv_rows].reshape(K + 1, inner + N) for side in (first, second)
    )
    conv_value_grad = jnp.concatenate([conv_first[:, :inner], conv_second[:, :inner]], 1)
    conv_state_grad = jnp.concatenate([conv_first[:, inner:], conv_second[:, inner:]], 1)
    at = at + conv_rows
    gated_rows = inner // LANES
    gated_gain_grad = jnp.concatenate(
        [first[at : at + gated_rows].reshape(inner), second[at : at + gated_rows].reshape(inner)]
    )
    at = at + gated_rows
    head_params_grad = jnp.concatenate(
        [first[at : at + 3, :heads], second[at : at + 3, :heads]], 1
    )

    value_weight_grad = mixed_reduced[:, :inner]
    this_state = mixed_reduced[:, inner:own_columns]
    other_state = swapped(this_state)
    first = jnp.where(model_index == 0, this_state, other_state)
    second = jnp.where(model_index == 0, other_state, this_state)
    state_weight_grad = jnp.concatenate(
        [first[:, :N], second[:, :N], first[:, N:], second[:, N:]], 1
    )
    new_value_velocity, value_update = matrix_momentum(value_weight_grad, value_weight_velocity)
    new_state_velocity, state_update = matrix_momentum(state_weight_grad, state_weight_velocity)
    value_grams = padded_to(head_grams(value_update), seq_count)
    per = value_grams.shape[0] // seq_count
    value_rows = per * P_SIZE * P_SIZE // LANES
    map_update = state_update[:, : 2 * N].reshape(-1, 2, N)
    step_update = state_update[:, 2 * N :]
    map_grams = jnp.einsum("rup,ruq->upq", map_update, map_update, precision=highest)
    step_gram = lax.dot_general(
        step_update, step_update, (((0,), (0,)), ((), ())), precision=highest
    )
    small = jnp.concatenate(
        [map_grams.reshape(2 * N, N), jnp.pad(step_gram, ((0, 0), (0, N - H)))], 0
    )
    summed, small_rows = gathered_sum(value_grams, small)
    value_own = chain(summed[:value_rows].reshape(per, P_SIZE, P_SIZE))
    value_poly, small = told_all(value_own, summed[value_rows:], value_rows, small_rows)
    state_poly = chain(
        jnp.stack(
            [small[:N], small[N : 2 * N], jnp.pad(small[2 * N : 2 * N + H], ((0, N - H), (0, 0)))]
        )
    )
    value_orth = apply_heads(value_update, value_poly[:heads])
    state_orth = jnp.concatenate(
        [
            jnp.einsum("rup,upq->ruq", map_update, state_poly[:2], precision=highest).reshape(
                -1, 2 * N
            ),
            jnp.dot(step_update, state_poly[2, :H, :H], precision=highest),
        ],
        1,
    )
    new_value_weight = value_weight - factor * value_orth
    new_state_weight = state_weight - factor * state_orth

    new_norm_gain, new_norm_velocity = vector_step(norm_gain, norm_gain_grad, norm_gain_velocity)
    new_conv_value, new_conv_value_velocity = vector_step(
        conv_value, conv_value_grad, conv_value_velocity
    )
    new_conv_state, new_conv_state_velocity = vector_step(
        conv_state, conv_state_grad, conv_state_velocity
    )
    new_head_params, new_head_velocity = vector_step(
        head_params, head_params_grad, head_params_velocity
    )
    new_gated_gain, new_gated_velocity = vector_step(
        gated_gain, gated_gain_grad, gated_gain_velocity
    )
    return (
        layer_output,
        input_grad,
        norm_gain_grad,
        gate_weight_grad,
        value_weight_grad,
        state_weight_grad,
        conv_value_grad,
        conv_state_grad,
        head_params_grad,
        gated_gain_grad,
        out_weight_grad,
        new_norm_gain,
        new_gate_weight,
        new_value_weight,
        new_state_weight,
        new_conv_value,
        new_conv_state,
        new_head_params,
        new_gated_gain,
        new_out_weight,
        new_norm_velocity,
        new_gate_velocity,
        new_value_velocity,
        new_state_velocity,
        new_conv_value_velocity,
        new_conv_state_velocity,
        new_head_velocity,
        new_gated_velocity,
        new_out_velocity,
    )


def solution(mesh):
    return jax.shard_map(
        body,
        mesh=mesh,
        in_specs=(
            P("seq", None),
            P("seq", None),
            P("seq"),
            P(),
            P("seq", "mp"),
            P("seq", "mp"),
            P("seq", None),
            P(),
            P(),
            P(),
            P(),
            P("seq", "mp"),
            P(),
            P("seq", "mp"),
            P("seq", "mp"),
            P("seq", None),
            P(),
            P(),
            P(),
            P(),
            P("seq", "mp"),
        ),
        out_specs=(
            P("seq", None),
            P("seq", None),
            P(),
            P("seq", "mp"),
            P("seq", "mp"),
            P("seq", None),
            P(),
            P(),
            P(),
            P(),
            P("seq", "mp"),
            P(),
            P("seq", "mp"),
            P("seq", "mp"),
            P("seq", None),
            P(),
            P(),
            P(),
            P(),
            P("seq", "mp"),
            P(),
            P("seq", "mp"),
            P("seq", "mp"),
            P("seq", None),
            P(),
            P(),
            P(),
            P(),
            P("seq", "mp"),
        ),
        check_vma=False,
    )
```

```python
import functools

import jax
import jax.numpy as jnp
from jax import lax
from jax.experimental import pallas as pl
from jax.experimental.layout import Layout, with_layout_constraint
from jax.experimental.pallas import tpu as pltpu
from jax.sharding import PartitionSpec as P

D = 1024
DI = 2048
H = 32
P_SIZE = 64
N = 128
K = 4
LANES = 128


highest = lax.Precision.HIGHEST
high = lax.Precision.HIGH
epsilon = 1e-05
momentum_decay = 0.95
matrix_rate = 0.03
vector_rate = 0.2
quintic_a = 3.4445
quintic_b = -4.775
quintic_c = 2.0315


def passed_along(shard, axis, by):
    size = lax.axis_size(axis)
    pairs = [(i, i + by) for i in range(size) if 0 <= i + by < size]
    return lax.ppermute(shard, axis, pairs)


def swapped(shard):
    return lax.ppermute(shard, "mp", [(0, 1), (1, 0)])


def pair_sum(shard):
    return shard + swapped(shard)


def exchange(array):
    return lax.all_to_all(array, "seq", 0, 0, tiled=True)


def matmul(left, right):
    return jnp.dot(left, right, precision=high)


def dot_last(left, right):
    return lax.dot_general(left, right, (((1,), (1,)), ((), ())), precision=high)


def dot_first(left, right):
    return lax.dot_general(left, right, (((0,), (0,)), ((), ())), precision=high)


def silu_slope(value):
    sigma = jax.nn.sigmoid(value)
    return sigma * (1.0 + value * (1.0 - sigma))


def carry_kernel(reverse, part_ref, out_ref):
    count, rows, _ = out_ref.shape

    def one(lap, state):
        source = count - 1 - lap if reverse else lap
        out_ref[source] = state
        return part_ref[source, rows : rows + 1] * state + part_ref[source, :rows]

    lax.fori_loop(0, count, one, jnp.zeros((rows, N), jnp.float32))


def carried_in(decay, state, reverse):
    count = lax.axis_size("seq")
    heads = state.shape[0]
    rows = heads * P_SIZE // count
    owner = jnp.repeat(decay, P_SIZE).reshape(count, rows)[:, :1]
    part = jnp.concatenate(
        [state.reshape(count, rows, N), jnp.broadcast_to(owner[:, :, None], (count, 8, N))], 1
    )
    gathered = exchange(part)
    entering = pl.pallas_call(
        functools.partial(carry_kernel, reverse),
        out_shape=jax.ShapeDtypeStruct((count, rows, N), jnp.float32),
        name="carry",
    )(gathered)
    return exchange(entering).reshape(heads, P_SIZE, N)


def chain_kernel(gram_ref, out_ref):
    count, size, _ = gram_ref.shape
    row = lax.broadcasted_iota(jnp.int32, (size, size), 0)
    col = lax.broadcasted_iota(jnp.int32, (size, size), 1)
    eye = (row == col).astype(jnp.float32)
    grams = []
    totals = []
    for unit in range(count):
        gram = gram_ref[unit]
        norm = jnp.sqrt(jnp.sum(gram * eye, keepdims=True)) + 1e-07
        grams.append(gram / (norm * norm))
        totals.append(eye / norm)
    for sweep in range(5):
        squares = [jnp.dot(gram, gram, precision=highest) for gram in grams]
        steps = [
            quintic_a * eye + quintic_b * gram + quintic_c * square
            for gram, square in zip(grams, squares)
        ]
        totals = [
            jnp.dot(total, step, precision=highest) for total, step in zip(totals, steps)
        ]
        if sweep < 4:
            halves = [
                jnp.dot(step, gram, precision=highest) for step, gram in zip(steps, grams)
            ]
            grams = [
                jnp.dot(half, step, precision=highest) for half, step in zip(halves, steps)
            ]
    for unit in range(count):
        out_ref[unit] = totals[unit]


def chain(grams):
    return pl.pallas_call(
        chain_kernel,
        out_shape=jax.ShapeDtypeStruct(grams.shape, jnp.float32),
        name="chain",
    )(grams)


def padded_to(array, multiple):
    extra = -array.shape[0] % multiple
    return jnp.pad(array, ((0, extra),) + ((0, 0),) * (array.ndim - 1))


def row_major(array):
    return with_layout_constraint(array, Layout(major_to_minor=(0, 1)))


def scatter_ready(parts):
    parts = [row_major(part) for part in parts]
    width = sum(part.shape[1] for part in parts)
    extra = -width % (3 * LANES)
    if extra:
        parts = parts + [jnp.zeros((parts[0].shape[0], extra), jnp.float32)]
    return jnp.concatenate(parts, 1)


def head_grams(update):
    split = update.reshape(update.shape[0], -1, P_SIZE)
    return jnp.einsum("rup,ruq->upq", split, split, precision=highest)


def apply_heads(update, polynomials):
    split = update.reshape(update.shape[0], -1, P_SIZE)
    return jnp.einsum("rup,upq->ruq", split, polynomials, precision=highest).reshape(update.shape)


def gathered_sum(grams, others):
    count = lax.axis_size("seq")
    others = padded_to(others, 8 * count)
    own_rows = others.shape[0] // count
    sent = jnp.concatenate(
        [grams.reshape(count, -1, LANES), others.reshape(count, own_rows, LANES)], 1
    )
    return jnp.sum(exchange(sent), 0), own_rows


def told_all(own, others, gram_rows, other_rows):
    count = lax.axis_size("seq")
    told = jnp.concatenate([own.reshape(gram_rows, LANES), others], 0)
    told = exchange(jnp.broadcast_to(told[None], (count,) + told.shape))
    return (
        told[:, :gram_rows].reshape(-1, P_SIZE, P_SIZE),
        told[:, gram_rows:].reshape(count * other_rows, LANES),
    )


def vector_step(current, gradient, velocity):
    new_velocity = momentum_decay * velocity + gradient
    direction = gradient + momentum_decay * new_velocity
    magnitude = jnp.sqrt(jnp.mean(current * current))
    return (
        current
        - vector_rate * magnitude * direction / jnp.sqrt(jnp.mean(direction * direction) + 1e-06),
        new_velocity,
    )


def matrix_momentum(gradient, velocity):
    new_velocity = momentum_decay * velocity + gradient
    return new_velocity, gradient + momentum_decay * new_velocity


def body(
    layer_input,
    cotangent,
    doc_starts,
    norm_gain,
    gate_weight,
    value_weight,
    state_weight,
    conv_value,
    conv_state,
    head_params,
    gated_gain,
    out_weight,
    norm_gain_velocity,
    gate_weight_velocity,
    value_weight_velocity,
    state_weight_velocity,
    conv_value_velocity,
    conv_state_velocity,
    head_params_velocity,
    gated_gain_velocity,
    out_weight_velocity,
):
    seq_count = lax.axis_size("seq")
    model_count = lax.axis_size("mp")
    model_index = lax.axis_index("mp")
    rows = layer_input.shape[0]
    inner = DI // model_count
    heads = H // model_count
    inner_start = model_index * inner
    head_start = model_index * heads
    rim = K - 1
    own_map = lax.dynamic_slice_in_dim(state_weight, model_index * N, N, 1)
    own_step = lax.dynamic_slice_in_dim(state_weight, 2 * N + head_start, heads, 1)
    mixed_full = lax.all_gather(
        jnp.concatenate([value_weight, own_map, own_step], 1), "seq", axis=0, tiled=True
    )
    outer_full = lax.all_gather(
        jnp.concatenate([gate_weight, out_weight], 1), "seq", axis=0, tiled=True
    )
    gain_local = lax.dynamic_slice_in_dim(gated_gain, inner_start, inner, 0)
    conv_local = jnp.concatenate(
        [
            lax.dynamic_slice_in_dim(conv_value, inner_start, inner, 1),
            lax.dynamic_slice_in_dim(conv_state, model_index * N, N, 1),
        ],
        1,
    )
    head_local = lax.dynamic_slice_in_dim(head_params, head_start, heads, 1)
    starts_float = doc_starts.astype(jnp.float32)
    scale = lax.rsqrt(jnp.mean(layer_input * layer_input, 1, keepdims=True) + epsilon)
    normed = layer_input * scale
    features = normed * norm_gain
    raw = jnp.dot(features, mixed_full, precision=highest)
    mixed_in = raw[:, : inner + N]
    prev_starts = passed_along(starts_float[rows - rim :], "seq", 1)
    prev_rows = passed_along(mixed_in[rows - rim :], "seq", 1)
    padded = jnp.concatenate([prev_rows, mixed_in], 0)
    cumulative = jnp.cumsum(jnp.concatenate([prev_starts, starts_float]))
    keeps = [jnp.ones((rows,), jnp.float32)]
    for lag in range(1, K):
        keeps.append(
            (cumulative[rim:] - cumulative[rim - lag : rim - lag + rows] < 0.5).astype(jnp.float32)
        )
    conv_pre = conv_local[K] + jnp.zeros_like(mixed_in)
    for lag in range(K):
        conv_pre = (
            conv_pre + keeps[lag][:, None] * conv_local[lag] * padded[rim - lag : rim - lag + rows]
        )
    activated = jax.nn.silu(conv_pre)
    head_values = activated[:, :inner].reshape(rows, heads, P_SIZE)
    this_map = activated[:, inner:]
    other_map = swapped(this_map)
    input_map = jnp.where(model_index == 0, this_map, other_map)
    read_map = jnp.where(model_index == 0, other_map, this_map)
    step_pre = raw[:, inner + N :] + head_local[0]
    step_size = jax.nn.softplus(step_pre)
    rate = -jnp.exp(head_local[1])
    skip = head_local[2]
    log_sums = jnp.cumsum(step_size * rate, 0)
    segment = jnp.cumsum(starts_float)
    position = jnp.arange(rows)
    causal_mask = (
        (position[:, None] >= position[None, :]) & (segment[:, None] == segment[None, :])
    )[None]
    head_logs = log_sums.T
    log_gap = head_logs[:, :, None] - head_logs[:, None, :]
    decay_mat = jnp.where(causal_mask, jnp.exp(jnp.where(causal_mask, log_gap, 0.0)), 0.0)
    scores = lax.dot_general(read_map, input_map, (((1,), (1,)), ((), ())), precision=highest)
    weighted = decay_mat * scores[None]
    scaled = head_values * step_size[..., None]
    last_log = log_sums[-1]
    last_segment = segment[-1]
    tail_weight = jnp.exp(last_log[None] - log_sums) * (segment == last_segment)[:, None]
    tail_scaled = scaled * tail_weight[..., None]
    block_state = jnp.einsum("jhp,jn->hpn", tail_scaled, input_map, precision=highest)
    block_decay = jnp.exp(last_log) * (last_segment == 0)
    entry_weight = jnp.exp(log_sums) * (segment == 0)[:, None]
    entries = carried_in(block_decay, block_state, False)
    intra = jnp.einsum("hij,jhp->ihp", weighted, scaled, precision=highest)
    state_read = jnp.einsum("hpn,in->ihp", entries, read_map, precision=highest)
    ssd_out = (
        intra + entry_weight[..., None] * state_read + head_values * skip[None, :, None]
    ).reshape(rows, inner)
    gate_full = outer_full[:, :inner]
    out_full = outer_full[:, inner:]
    gate = matmul(features, gate_full)
    grad_gated = matmul(cotangent, out_full)
    grad_hat = grad_gated * gain_local
    gate_act = jax.nn.silu(gate)
    product = ssd_out * gate_act
    row_sums = pair_sum(jnp.stack([jnp.sum(product * product, 1), jnp.sum(product * grad_hat, 1)]))
    gate_scale = lax.rsqrt(row_sums[0] / DI + epsilon)[:, None]
    inner_sum = row_sums[1][:, None]
    gated = product * gate_scale * gain_local
    grad_product = gate_scale * (grad_hat - product * gate_scale * gate_scale * (inner_sum / DI))
    grad_gate = grad_product * ssd_out * silu_slope(gate)
    outer_partial = scatter_ready([dot_first(features, grad_gate), dot_first(cotangent, gated)])
    outer_partial, grad_product = lax.optimization_barrier((outer_partial, grad_product))
    outer_reduced = lax.psum_scatter(outer_partial, "seq", scatter_dimension=0, tiled=True)
    layer_output = layer_input + pair_sum(dot_last(gated, out_full))
    gated_gain_part = jnp.sum(grad_gated * product * gate_scale, 0)
    ssd_grad = (grad_product * gate_act).reshape(rows, heads, P_SIZE)
    skip_grad = jnp.sum(ssd_grad * head_values, (0, 2))
    weighted_grad = ssd_grad * entry_weight[..., None]
    enter_grad = jnp.einsum("ihp,in->hpn", weighted_grad, read_map, precision=highest)
    out_grads = carried_in(block_decay, enter_grad, True)
    read_grad = jnp.einsum("ihp,hpn->in", weighted_grad, entries, precision=highest)
    logs_grad = jnp.sum(ssd_grad * state_read, 2) * entry_weight
    mix_grad = jnp.einsum("ihp,jhp->hij", ssd_grad, scaled, precision=highest)
    scaled_grad = jnp.einsum("hij,ihp->jhp", weighted, ssd_grad, precision=highest)
    score_grad = jnp.sum(mix_grad * decay_mat, 0)
    read_grad = read_grad + jnp.dot(score_grad, input_map, precision=highest)
    input_grad_map = lax.dot_general(
        score_grad, read_map, (((0,), (0,)), ((), ())), precision=highest
    )
    decay_term = mix_grad * weighted
    logs_grad = logs_grad + (jnp.sum(decay_term, 2) - jnp.sum(decay_term, 1)).T
    from_state = jnp.einsum("hpn,jn->jhp", out_grads, input_map, precision=highest)
    scaled_grad = scaled_grad + tail_weight[..., None] * from_state
    input_grad_map = input_grad_map + jnp.einsum(
        "hpn,jhp->jn", out_grads, tail_scaled, precision=highest
    )
    tail_grad = jnp.sum(from_state * tail_scaled, 2)
    last_grad = jnp.sum(tail_grad, 0) + jnp.sum(out_grads * entries, (1, 2)) * block_decay
    logs_grad = logs_grad - tail_grad
    decay_log_grad = jnp.flip(jnp.cumsum(jnp.flip(logs_grad, 0), 0), 0) + last_grad[None]
    grad_values = ssd_grad * skip[None, :, None] + scaled_grad * step_size[..., None]
    step_grad = jnp.sum(scaled_grad * head_values, 2) + decay_log_grad * rate
    rate_grad = jnp.sum(decay_log_grad * step_size, 0)
    log_rate_grad = rate_grad * rate
    step_pre_grad = step_grad * jax.nn.sigmoid(step_pre)
    bias_grad = jnp.sum(step_pre_grad, 0)
    this_grad = jnp.where(model_index == 0, input_grad_map, read_grad)
    other_grad = jnp.where(model_index == 0, read_grad, input_grad_map)
    act_grad = jnp.concatenate(
        [grad_values.reshape(rows, inner), this_grad + swapped(other_grad)], 1
    )
    pre_grad = act_grad * silu_slope(conv_pre)
    conv_rows = []
    padded_grad = jnp.zeros_like(padded)
    for lag in range(K):
        masked = keeps[lag][:, None] * pre_grad
        conv_rows.append(jnp.sum(masked * padded[rim - lag : rim - lag + rows], 0))
        padded_grad = padded_grad + jnp.pad(masked * conv_local[lag], ((rim - lag, lag), (0, 0)))
    conv_rows.append(jnp.sum(pre_grad, 0))
    conv_local_grad = jnp.stack(conv_rows)
    spill = passed_along(padded_grad[:rim], "seq", -1)
    mixed_grad = padded_grad[rim:] + jnp.pad(spill, ((rows - rim, 0), (0, 0)))
    raw_grad = jnp.concatenate([mixed_grad, step_pre_grad], 1)
    mixed_partial = scatter_ready([dot_first(features, mixed_grad)])
    step_partial = dot_first(features, step_pre_grad)
    mixed_partial, raw_grad, outer_reduced = lax.optimization_barrier(
        (mixed_partial, raw_grad, outer_reduced)
    )
    mixed_reduced = lax.psum_scatter(mixed_partial, "seq", scatter_dimension=0, tiled=True)
    features_grad = pair_sum(dot_last(grad_gate, gate_full) + dot_last(raw_grad, mixed_full))
    norm_gain_part = jnp.sum(features_grad * normed, 0)
    gain_grad_in = features_grad * norm_gain
    input_grad = cotangent + scale * (
        gain_grad_in - normed * jnp.mean(gain_grad_in * normed, 1, keepdims=True)
    )

    factor = matrix_rate * 0.2 * D**0.5
    gate_weight_grad = outer_reduced[:, :inner]
    out_weight_grad = outer_reduced[:, inner : 2 * inner]
    new_gate_velocity, gate_update = matrix_momentum(gate_weight_grad, gate_weight_velocity)
    new_out_velocity, out_update = matrix_momentum(out_weight_grad, out_weight_velocity)
    outer_update = jnp.concatenate([gate_update, out_update], 1)
    outer_grams = padded_to(head_grams(outer_update), seq_count)
    per = outer_grams.shape[0] // seq_count
    outer_rows = per * P_SIZE * P_SIZE // LANES
    vectors = jnp.concatenate(
        [
            norm_gain_part.reshape(-1, LANES),
            conv_local_grad.reshape(-1, LANES),
            gated_gain_part.reshape(-1, LANES),
            jnp.pad(jnp.stack([bias_grad, log_rate_grad, skip_grad]), ((0, 0), (0, LANES - heads))),
        ],
        0,
    )
    step_rows = D * heads // LANES // seq_count
    summed, vector_rows = gathered_sum(
        jnp.concatenate(
            [
                outer_grams.reshape(seq_count, outer_rows, LANES),
                step_partial.reshape(seq_count, step_rows, LANES),
            ],
            1,
        ),
        vectors,
    )
    this_step = summed[outer_rows : outer_rows + step_rows].reshape(-1, heads)
    outer_own = chain(summed[:outer_rows].reshape(per, P_SIZE, P_SIZE))
    outer_poly, vectors = told_all(
        outer_own, summed[outer_rows + step_rows :], outer_rows, vector_rows
    )
    mixed_reduced, outer_poly = lax.optimization_barrier((mixed_reduced, outer_poly))
    outer_orth = apply_heads(outer_update, outer_poly[: 2 * heads])
    new_gate_weight = gate_weight - factor * outer_orth[:, :inner]
    new_out_weight = out_weight - factor * outer_orth[:, inner:]

    at = D // LANES
    norm_gain_grad = vectors[:at].reshape(D)
    other = swapped(vectors)
    first = jnp.where(model_index == 0, vectors, other)
    second = jnp.where(model_index == 0, other, vectors)
    conv_rows = (K + 1) * (inner + N) // LANES
    conv_first, conv_second = (
        side[at : at + conv_rows].reshape(K + 1, inner + N) for side in (first, second)
    )
    conv_value_grad = jnp.concatenate([conv_first[:, :inner], conv_second[:, :inner]], 1)
    conv_state_grad = jnp.concatenate([conv_first[:, inner:], conv_second[:, inner:]], 1)
    at = at + conv_rows
    gated_rows = inner // LANES
    gated_gain_grad = jnp.concatenate(
        [first[at : at + gated_rows].reshape(inner), second[at : at + gated_rows].reshape(inner)]
    )
    at = at + gated_rows
    head_params_grad = jnp.concatenate(
        [first[at : at + 3, :heads], second[at : at + 3, :heads]], 1
    )

    value_weight_grad = mixed_reduced[:, :inner]
    this_state = jnp.concatenate([mixed_reduced[:, inner : inner + N], this_step], 1)
    other_state = swapped(this_state)
    first = jnp.where(model_index == 0, this_state, other_state)
    second = jnp.where(model_index == 0, other_state, this_state)
    state_weight_grad = jnp.concatenate(
        [first[:, :N], second[:, :N], first[:, N:], second[:, N:]], 1
    )
    new_value_velocity, value_update = matrix_momentum(value_weight_grad, value_weight_velocity)
    new_state_velocity, state_update = matrix_momentum(state_weight_grad, state_weight_velocity)
    value_grams = padded_to(head_grams(value_update), seq_count)
    per = value_grams.shape[0] // seq_count
    value_rows = per * P_SIZE * P_SIZE // LANES
    map_update = state_update[:, : 2 * N].reshape(-1, 2, N)
    step_update = state_update[:, 2 * N :]
    map_grams = jnp.einsum("rup,ruq->upq", map_update, map_update, precision=highest)
    step_gram = lax.dot_general(
        step_update, step_update, (((0,), (0,)), ((), ())), precision=highest
    )
    small = jnp.concatenate(
        [map_grams.reshape(2 * N, N), jnp.pad(step_gram, ((0, 0), (0, N - H)))], 0
    )
    summed, small_rows = gathered_sum(value_grams, small)
    value_own = chain(summed[:value_rows].reshape(per, P_SIZE, P_SIZE))
    value_poly, small = told_all(value_own, summed[value_rows:], value_rows, small_rows)
    state_poly = chain(
        jnp.stack(
            [small[:N], small[N : 2 * N], jnp.pad(small[2 * N : 2 * N + H], ((0, N - H), (0, 0)))]
        )
    )
    value_orth = apply_heads(value_update, value_poly[:heads])
    state_orth = jnp.concatenate(
        [
            jnp.einsum("rup,upq->ruq", map_update, state_poly[:2], precision=highest).reshape(
                -1, 2 * N
            ),
            jnp.dot(step_update, state_poly[2, :H, :H], precision=highest),
        ],
        1,
    )
    new_value_weight = value_weight - factor * value_orth
    new_state_weight = state_weight - factor * state_orth

    new_norm_gain, new_norm_velocity = vector_step(norm_gain, norm_gain_grad, norm_gain_velocity)
    new_conv_value, new_conv_value_velocity = vector_step(
        conv_value, conv_value_grad, conv_value_velocity
    )
    new_conv_state, new_conv_state_velocity = vector_step(
        conv_state, conv_state_grad, conv_state_velocity
    )
    new_head_params, new_head_velocity = vector_step(
        head_params, head_params_grad, head_params_velocity
    )
    new_gated_gain, new_gated_velocity = vector_step(
        gated_gain, gated_gain_grad, gated_gain_velocity
    )
    return (
        layer_output,
        input_grad,
        norm_gain_grad,
        gate_weight_grad,
        value_weight_grad,
        state_weight_grad,
        conv_value_grad,
        conv_state_grad,
        head_params_grad,
        gated_gain_grad,
        out_weight_grad,
        new_norm_gain,
        new_gate_weight,
        new_value_weight,
        new_state_weight,
        new_conv_value,
        new_conv_state,
        new_head_params,
        new_gated_gain,
        new_out_weight,
        new_norm_velocity,
        new_gate_velocity,
        new_value_velocity,
        new_state_velocity,
        new_conv_value_velocity,
        new_conv_state_velocity,
        new_head_velocity,
        new_gated_velocity,
        new_out_velocity,
    )


def solution(mesh):
    return jax.shard_map(
        body,
        mesh=mesh,
        in_specs=(
            P("seq", None),
            P("seq", None),
            P("seq"),
            P(),
            P("seq", "mp"),
            P("seq", "mp"),
            P("seq", None),
            P(),
            P(),
            P(),
            P(),
            P("seq", "mp"),
            P(),
            P("seq", "mp"),
            P("seq", "mp"),
            P("seq", None),
            P(),
            P(),
            P(),
            P(),
            P("seq", "mp"),
        ),
        out_specs=(
            P("seq", None),
            P("seq", None),
            P(),
            P("seq", "mp"),
            P("seq", "mp"),
            P("seq", None),
            P(),
            P(),
            P(),
            P(),
            P("seq", "mp"),
            P(),
            P("seq", "mp"),
            P("seq", "mp"),
            P("seq", None),
            P(),
            P(),
            P(),
            P(),
            P("seq", "mp"),
            P(),
            P("seq", "mp"),
            P("seq", "mp"),
            P("seq", None),
            P(),
            P(),
            P(),
            P(),
            P("seq", "mp"),
        ),
        check_vma=False,
    )
```

```python
import functools

import jax
import jax.numpy as jnp
from jax import lax
from jax.experimental import pallas as pl
from jax.experimental.layout import Layout, with_layout_constraint
from jax.experimental.pallas import tpu as pltpu
from jax.sharding import PartitionSpec as P

D = 1024
DI = 2048
H = 32
P_SIZE = 64
N = 128
K = 4
LANES = 128


highest = lax.Precision.HIGHEST
high = lax.Precision.HIGH
epsilon = 1e-05
momentum_decay = 0.95
matrix_rate = 0.03
vector_rate = 0.2
quintic_a = 3.4445
quintic_b = -4.775
quintic_c = 2.0315


def passed_along(shard, axis, by):
    size = lax.axis_size(axis)
    pairs = [(i, i + by) for i in range(size) if 0 <= i + by < size]
    return lax.ppermute(shard, axis, pairs)


def swapped(shard):
    return lax.ppermute(shard, "mp", [(0, 1), (1, 0)])


def pair_sum(shard):
    return shard + swapped(shard)


def exchange(array):
    return lax.all_to_all(array, "seq", 0, 0, tiled=True)


def matmul(left, right):
    return jnp.dot(left, right, precision=high)


def dot_last(left, right):
    return lax.dot_general(left, right, (((1,), (1,)), ((), ())), precision=high)


def dot_first(left, right):
    return lax.dot_general(left, right, (((0,), (0,)), ((), ())), precision=high)


def silu_slope(value):
    sigma = jax.nn.sigmoid(value)
    return sigma * (1.0 + value * (1.0 - sigma))


def carry_kernel(reverse, part_ref, out_ref):
    count, rows, _ = out_ref.shape

    def one(lap, state):
        source = count - 1 - lap if reverse else lap
        out_ref[source] = state
        return part_ref[source, rows : rows + 1] * state + part_ref[source, :rows]

    lax.fori_loop(0, count, one, jnp.zeros((rows, N), jnp.float32))


def carried_in(decay, state, reverse):
    count = lax.axis_size("seq")
    heads = state.shape[0]
    rows = heads * P_SIZE // count
    owner = jnp.repeat(decay, P_SIZE).reshape(count, rows)[:, :1]
    part = jnp.concatenate(
        [state.reshape(count, rows, N), jnp.broadcast_to(owner[:, :, None], (count, 8, N))], 1
    )
    gathered = exchange(part)
    entering = pl.pallas_call(
        functools.partial(carry_kernel, reverse),
        out_shape=jax.ShapeDtypeStruct((count, rows, N), jnp.float32),
        name="carry",
    )(gathered)
    return exchange(entering).reshape(heads, P_SIZE, N)


def chain_kernel(gram_ref, out_ref):
    count, size, _ = gram_ref.shape
    row = lax.broadcasted_iota(jnp.int32, (size, size), 0)
    col = lax.broadcasted_iota(jnp.int32, (size, size), 1)
    eye = (row == col).astype(jnp.float32)
    grams = []
    totals = []
    for unit in range(count):
        gram = gram_ref[unit]
        norm = jnp.sqrt(jnp.sum(gram * eye, keepdims=True)) + 1e-07
        grams.append(gram / (norm * norm))
        totals.append(eye / norm)
    for sweep in range(5):
        squares = [jnp.dot(gram, gram, precision=highest) for gram in grams]
        steps = [
            quintic_a * eye + quintic_b * gram + quintic_c * square
            for gram, square in zip(grams, squares)
        ]
        totals = [
            jnp.dot(total, step, precision=highest) for total, step in zip(totals, steps)
        ]
        if sweep < 4:
            halves = [
                jnp.dot(step, gram, precision=highest) for step, gram in zip(steps, grams)
            ]
            grams = [
                jnp.dot(half, step, precision=highest) for half, step in zip(halves, steps)
            ]
    for unit in range(count):
        out_ref[unit] = totals[unit]


def chain(grams):
    return pl.pallas_call(
        chain_kernel,
        out_shape=jax.ShapeDtypeStruct(grams.shape, jnp.float32),
        name="chain",
    )(grams)


def padded_to(array, multiple):
    extra = -array.shape[0] % multiple
    return jnp.pad(array, ((0, extra),) + ((0, 0),) * (array.ndim - 1))


def row_major(array):
    return with_layout_constraint(array, Layout(major_to_minor=(0, 1)))


def rows_sum(array, width):
    gathered = exchange(array)
    return jnp.sum(gathered.reshape(lax.axis_size("seq"), -1, width), 0)


def head_grams(update):
    split = update.reshape(update.shape[0], -1, P_SIZE)
    return jnp.einsum("rup,ruq->upq", split, split, precision=highest)


def apply_heads(update, polynomials):
    split = update.reshape(update.shape[0], -1, P_SIZE)
    return jnp.einsum("rup,upq->ruq", split, polynomials, precision=highest).reshape(update.shape)


def gathered_sum(grams, others):
    count = lax.axis_size("seq")
    others = padded_to(others, 8 * count)
    own_rows = others.shape[0] // count
    sent = jnp.concatenate(
        [grams.reshape(count, -1, LANES), others.reshape(count, own_rows, LANES)], 1
    )
    return jnp.sum(exchange(sent), 0), own_rows


def told_all(own, others, gram_rows, other_rows):
    count = lax.axis_size("seq")
    told = jnp.concatenate([own.reshape(gram_rows, LANES), others], 0)
    told = exchange(jnp.broadcast_to(told[None], (count,) + told.shape))
    return (
        told[:, :gram_rows].reshape(-1, P_SIZE, P_SIZE),
        told[:, gram_rows:].reshape(count * other_rows, LANES),
    )


def vector_step(current, gradient, velocity):
    new_velocity = momentum_decay * velocity + gradient
    direction = gradient + momentum_decay * new_velocity
    magnitude = jnp.sqrt(jnp.mean(current * current))
    return (
        current
        - vector_rate * magnitude * direction / jnp.sqrt(jnp.mean(direction * direction) + 1e-06),
        new_velocity,
    )


def matrix_momentum(gradient, velocity):
    new_velocity = momentum_decay * velocity + gradient
    return new_velocity, gradient + momentum_decay * new_velocity


def body(
    layer_input,
    cotangent,
    doc_starts,
    norm_gain,
    gate_weight,
    value_weight,
    state_weight,
    conv_value,
    conv_state,
    head_params,
    gated_gain,
    out_weight,
    norm_gain_velocity,
    gate_weight_velocity,
    value_weight_velocity,
    state_weight_velocity,
    conv_value_velocity,
    conv_state_velocity,
    head_params_velocity,
    gated_gain_velocity,
    out_weight_velocity,
):
    seq_count = lax.axis_size("seq")
    model_count = lax.axis_size("mp")
    model_index = lax.axis_index("mp")
    rows = layer_input.shape[0]
    inner = DI // model_count
    heads = H // model_count
    inner_start = model_index * inner
    head_start = model_index * heads
    rim = K - 1
    own_map = lax.dynamic_slice_in_dim(state_weight, model_index * N, N, 1)
    own_step = lax.dynamic_slice_in_dim(state_weight, 2 * N + head_start, heads, 1)
    mixed_full = lax.all_gather(
        jnp.concatenate([value_weight, own_map, own_step], 1), "seq", axis=0, tiled=True
    )
    outer_full = lax.all_gather(
        jnp.concatenate([gate_weight, out_weight], 1), "seq", axis=0, tiled=True
    )
    gain_local = lax.dynamic_slice_in_dim(gated_gain, inner_start, inner, 0)
    conv_local = jnp.concatenate(
        [
            lax.dynamic_slice_in_dim(conv_value, inner_start, inner, 1),
            lax.dynamic_slice_in_dim(conv_state, model_index * N, N, 1),
        ],
        1,
    )
    head_local = lax.dynamic_slice_in_dim(head_params, head_start, heads, 1)
    starts_float = doc_starts.astype(jnp.float32)
    scale = lax.rsqrt(jnp.mean(layer_input * layer_input, 1, keepdims=True) + epsilon)
    normed = layer_input * scale
    features = normed * norm_gain
    raw = jnp.dot(features, mixed_full, precision=highest)
    mixed_in = raw[:, : inner + N]
    prev_starts = passed_along(starts_float[rows - rim :], "seq", 1)
    prev_rows = passed_along(mixed_in[rows - rim :], "seq", 1)
    padded = jnp.concatenate([prev_rows, mixed_in], 0)
    cumulative = jnp.cumsum(jnp.concatenate([prev_starts, starts_float]))
    keeps = [jnp.ones((rows,), jnp.float32)]
    for lag in range(1, K):
        keeps.append(
            (cumulative[rim:] - cumulative[rim - lag : rim - lag + rows] < 0.5).astype(jnp.float32)
        )
    conv_pre = conv_local[K] + jnp.zeros_like(mixed_in)
    for lag in range(K):
        conv_pre = (
            conv_pre + keeps[lag][:, None] * conv_local[lag] * padded[rim - lag : rim - lag + rows]
        )
    activated = jax.nn.silu(conv_pre)
    head_values = activated[:, :inner].reshape(rows, heads, P_SIZE)
    this_map = activated[:, inner:]
    other_map = swapped(this_map)
    input_map = jnp.where(model_index == 0, this_map, other_map)
    read_map = jnp.where(model_index == 0, other_map, this_map)
    step_pre = raw[:, inner + N :] + head_local[0]
    step_size = jax.nn.softplus(step_pre)
    rate = -jnp.exp(head_local[1])
    skip = head_local[2]
    log_sums = jnp.cumsum(step_size * rate, 0)
    segment = jnp.cumsum(starts_float)
    position = jnp.arange(rows)
    causal_mask = (
        (position[:, None] >= position[None, :]) & (segment[:, None] == segment[None, :])
    )[None]
    head_logs = log_sums.T
    log_gap = head_logs[:, :, None] - head_logs[:, None, :]
    decay_mat = jnp.where(causal_mask, jnp.exp(jnp.where(causal_mask, log_gap, 0.0)), 0.0)
    scores = lax.dot_general(read_map, input_map, (((1,), (1,)), ((), ())), precision=highest)
    weighted = decay_mat * scores[None]
    scaled = head_values * step_size[..., None]
    last_log = log_sums[-1]
    last_segment = segment[-1]
    tail_weight = jnp.exp(last_log[None] - log_sums) * (segment == last_segment)[:, None]
    tail_scaled = scaled * tail_weight[..., None]
    block_state = jnp.einsum("jhp,jn->hpn", tail_scaled, input_map, precision=highest)
    block_decay = jnp.exp(last_log) * (last_segment == 0)
    entry_weight = jnp.exp(log_sums) * (segment == 0)[:, None]
    entries = carried_in(block_decay, block_state, False)
    intra = jnp.einsum("hij,jhp->ihp", weighted, scaled, precision=highest)
    state_read = jnp.einsum("hpn,in->ihp", entries, read_map, precision=highest)
    ssd_out = (
        intra + entry_weight[..., None] * state_read + head_values * skip[None, :, None]
    ).reshape(rows, inner)
    gate_full = outer_full[:, :inner]
    out_full = outer_full[:, inner:]
    gate = matmul(features, gate_full)
    grad_gated = matmul(cotangent, out_full)
    grad_hat = grad_gated * gain_local
    gate_act = jax.nn.silu(gate)
    product = ssd_out * gate_act
    row_sums = pair_sum(jnp.stack([jnp.sum(product * product, 1), jnp.sum(product * grad_hat, 1)]))
    gate_scale = lax.rsqrt(row_sums[0] / DI + epsilon)[:, None]
    inner_sum = row_sums[1][:, None]
    gated = product * gate_scale * gain_local
    grad_product = gate_scale * (grad_hat - product * gate_scale * gate_scale * (inner_sum / DI))
    grad_gate = grad_product * ssd_out * silu_slope(gate)
    early = 5 * inner // 8
    outer_partial = jnp.concatenate(
        [
            row_major(dot_first(features, grad_gate)),
            row_major(dot_first(cotangent, gated[:, :early])),
        ],
        1,
    )
    outer_partial, grad_product = lax.optimization_barrier((outer_partial, grad_product))
    outer_reduced = lax.psum_scatter(outer_partial, "seq", scatter_dimension=0, tiled=True)
    layer_output = layer_input + pair_sum(dot_last(gated, out_full))
    gated_gain_part = jnp.sum(grad_gated * product * gate_scale, 0)
    ssd_grad = (grad_product * gate_act).reshape(rows, heads, P_SIZE)
    skip_grad = jnp.sum(ssd_grad * head_values, (0, 2))
    weighted_grad = ssd_grad * entry_weight[..., None]
    enter_grad = jnp.einsum("ihp,in->hpn", weighted_grad, read_map, precision=highest)
    out_grads = carried_in(block_decay, enter_grad, True)
    late_partial = row_major(dot_first(cotangent, gated[:, early:]))
    late_partial, out_grads = lax.optimization_barrier((late_partial, out_grads))
    late_reduced = rows_sum(late_partial, inner - early)
    read_grad = jnp.einsum("ihp,hpn->in", weighted_grad, entries, precision=highest)
    logs_grad = jnp.sum(ssd_grad * state_read, 2) * entry_weight
    mix_grad = jnp.einsum("ihp,jhp->hij", ssd_grad, scaled, precision=highest)
    scaled_grad = jnp.einsum("hij,ihp->jhp", weighted, ssd_grad, precision=highest)
    score_grad = jnp.sum(mix_grad * decay_mat, 0)
    read_grad = read_grad + jnp.dot(score_grad, input_map, precision=highest)
    input_grad_map = lax.dot_general(
        score_grad, read_map, (((0,), (0,)), ((), ())), precision=highest
    )
    decay_term = mix_grad * weighted
    logs_grad = logs_grad + (jnp.sum(decay_term, 2) - jnp.sum(decay_term, 1)).T
    from_state = jnp.einsum("hpn,jn->jhp", out_grads, input_map, precision=highest)
    scaled_grad = scaled_grad + tail_weight[..., None] * from_state
    input_grad_map = input_grad_map + jnp.einsum(
        "hpn,jhp->jn", out_grads, tail_scaled, precision=highest
    )
    tail_grad = jnp.sum(from_state * tail_scaled, 2)
    last_grad = jnp.sum(tail_grad, 0) + jnp.sum(out_grads * entries, (1, 2)) * block_decay
    logs_grad = logs_grad - tail_grad
    decay_log_grad = jnp.flip(jnp.cumsum(jnp.flip(logs_grad, 0), 0), 0) + last_grad[None]
    grad_values = ssd_grad * skip[None, :, None] + scaled_grad * step_size[..., None]
    step_grad = jnp.sum(scaled_grad * head_values, 2) + decay_log_grad * rate
    rate_grad = jnp.sum(decay_log_grad * step_size, 0)
    log_rate_grad = rate_grad * rate
    step_pre_grad = step_grad * jax.nn.sigmoid(step_pre)
    bias_grad = jnp.sum(step_pre_grad, 0)
    this_grad = jnp.where(model_index == 0, input_grad_map, read_grad)
    other_grad = jnp.where(model_index == 0, read_grad, input_grad_map)
    act_grad = jnp.concatenate(
        [grad_values.reshape(rows, inner), this_grad + swapped(other_grad)], 1
    )
    pre_grad = act_grad * silu_slope(conv_pre)
    conv_rows = []
    padded_grad = jnp.zeros_like(padded)
    for lag in range(K):
        masked = keeps[lag][:, None] * pre_grad
        conv_rows.append(jnp.sum(masked * padded[rim - lag : rim - lag + rows], 0))
        padded_grad = padded_grad + jnp.pad(masked * conv_local[lag], ((rim - lag, lag), (0, 0)))
    conv_rows.append(jnp.sum(pre_grad, 0))
    conv_local_grad = jnp.stack(conv_rows)
    spill = passed_along(padded_grad[:rim], "seq", -1)
    mixed_grad = padded_grad[rim:] + jnp.pad(spill, ((rows - rim, 0), (0, 0)))
    raw_grad = jnp.concatenate([mixed_grad, step_pre_grad], 1)
    mixed_partial = row_major(dot_first(features, mixed_grad[:, :inner]))
    map_partial = row_major(dot_first(features, mixed_grad[:, inner:]))
    step_partial = dot_first(features, step_pre_grad)
    mixed_partial, raw_grad, map_partial = lax.optimization_barrier(
        (mixed_partial, raw_grad, map_partial)
    )
    step_rows = D * heads // LANES // seq_count
    state_sums = rows_sum(
        jnp.concatenate(
            [
                map_partial.reshape(seq_count, -1, LANES),
                step_partial.reshape(seq_count, step_rows, LANES),
            ],
            1,
        ),
        LANES,
    )
    raw_grad, late_reduced, state_sums = lax.optimization_barrier(
        (raw_grad, late_reduced, state_sums)
    )
    mixed_reduced = lax.psum_scatter(mixed_partial, "seq", scatter_dimension=0, tiled=True)
    features_grad = pair_sum(dot_last(grad_gate, gate_full) + dot_last(raw_grad, mixed_full))
    norm_gain_part = jnp.sum(features_grad * normed, 0)
    gain_grad_in = features_grad * norm_gain
    input_grad = cotangent + scale * (
        gain_grad_in - normed * jnp.mean(gain_grad_in * normed, 1, keepdims=True)
    )

    factor = matrix_rate * 0.2 * D**0.5
    gate_weight_grad = outer_reduced[:, :inner]
    out_weight_grad = jnp.concatenate([outer_reduced[:, inner:], late_reduced], 1)
    new_gate_velocity, gate_update = matrix_momentum(gate_weight_grad, gate_weight_velocity)
    new_out_velocity, out_update = matrix_momentum(out_weight_grad, out_weight_velocity)
    outer_update = jnp.concatenate([gate_update, out_update], 1)
    outer_grams = padded_to(head_grams(outer_update), seq_count)
    per = outer_grams.shape[0] // seq_count
    outer_rows = per * P_SIZE * P_SIZE // LANES
    this_state = jnp.concatenate(
        [state_sums[:-step_rows], state_sums[-step_rows:].reshape(-1, heads)], 1
    )
    other_state = swapped(this_state)
    first = jnp.where(model_index == 0, this_state, other_state)
    second = jnp.where(model_index == 0, other_state, this_state)
    state_weight_grad = jnp.concatenate(
        [first[:, :N], second[:, :N], first[:, N:], second[:, N:]], 1
    )
    new_state_velocity, state_update = matrix_momentum(state_weight_grad, state_weight_velocity)
    map_update = state_update[:, : 2 * N].reshape(-1, 2, N)
    step_update = state_update[:, 2 * N :]
    map_grams = jnp.einsum("rup,ruq->upq", map_update, map_update, precision=highest)
    step_gram = lax.dot_general(
        step_update, step_update, (((0,), (0,)), ((), ())), precision=highest
    )
    others = jnp.concatenate(
        [
            map_grams.reshape(2 * N, N),
            jnp.pad(step_gram, ((0, 0), (0, N - H))),
            norm_gain_part.reshape(-1, LANES),
            conv_local_grad.reshape(-1, LANES),
            gated_gain_part.reshape(-1, LANES),
            jnp.pad(jnp.stack([bias_grad, log_rate_grad, skip_grad]), ((0, 0), (0, LANES - heads))),
        ],
        0,
    )
    summed, other_rows = gathered_sum(outer_grams, others)
    outer_own = chain(summed[:outer_rows].reshape(per, P_SIZE, P_SIZE))
    outer_poly, others = told_all(outer_own, summed[outer_rows:], outer_rows, other_rows)
    mixed_reduced, outer_poly = lax.optimization_barrier((mixed_reduced, outer_poly))
    outer_orth = apply_heads(outer_update, outer_poly[: 2 * heads])
    new_gate_weight = gate_weight - factor * outer_orth[:, :inner]
    new_out_weight = out_weight - factor * outer_orth[:, inner:]
    state_poly = chain(
        jnp.stack(
            [
                others[:N],
                others[N : 2 * N],
                jnp.pad(others[2 * N : 2 * N + H], ((0, N - H), (0, 0))),
            ]
        )
    )
    state_orth = jnp.concatenate(
        [
            jnp.einsum("rup,upq->ruq", map_update, state_poly[:2], precision=highest).reshape(
                -1, 2 * N
            ),
            jnp.dot(step_update, state_poly[2, :H, :H], precision=highest),
        ],
        1,
    )
    new_state_weight = state_weight - factor * state_orth

    vectors = others[2 * N + H :]
    at = D // LANES
    norm_gain_grad = vectors[:at].reshape(D)
    other = swapped(vectors)
    first = jnp.where(model_index == 0, vectors, other)
    second = jnp.where(model_index == 0, other, vectors)
    conv_rows = (K + 1) * (inner + N) // LANES
    conv_first, conv_second = (
        side[at : at + conv_rows].reshape(K + 1, inner + N) for side in (first, second)
    )
    conv_value_grad = jnp.concatenate([conv_first[:, :inner], conv_second[:, :inner]], 1)
    conv_state_grad = jnp.concatenate([conv_first[:, inner:], conv_second[:, inner:]], 1)
    at = at + conv_rows
    gated_rows = inner // LANES
    gated_gain_grad = jnp.concatenate(
        [first[at : at + gated_rows].reshape(inner), second[at : at + gated_rows].reshape(inner)]
    )
    at = at + gated_rows
    head_params_grad = jnp.concatenate(
        [first[at : at + 3, :heads], second[at : at + 3, :heads]], 1
    )

    value_weight_grad = mixed_reduced
    new_value_velocity, value_update = matrix_momentum(value_weight_grad, value_weight_velocity)
    value_grams = padded_to(head_grams(value_update), seq_count)
    per = value_grams.shape[0] // seq_count
    value_rows = per * P_SIZE * P_SIZE // LANES
    summed = jnp.sum(exchange(value_grams.reshape(seq_count, value_rows, LANES)), 0)
    value_own = chain(summed.reshape(per, P_SIZE, P_SIZE)).reshape(value_rows, LANES)
    told = exchange(jnp.broadcast_to(value_own[None], (seq_count, value_rows, LANES)))
    value_poly = told.reshape(-1, P_SIZE, P_SIZE)[:heads]
    value_orth = apply_heads(value_update, value_poly)
    new_value_weight = value_weight - factor * value_orth

    new_norm_gain, new_norm_velocity = vector_step(norm_gain, norm_gain_grad, norm_gain_velocity)
    new_conv_value, new_conv_value_velocity = vector_step(
        conv_value, conv_value_grad, conv_value_velocity
    )
    new_conv_state, new_conv_state_velocity = vector_step(
        conv_state, conv_state_grad, conv_state_velocity
    )
    new_head_params, new_head_velocity = vector_step(
        head_params, head_params_grad, head_params_velocity
    )
    new_gated_gain, new_gated_velocity = vector_step(
        gated_gain, gated_gain_grad, gated_gain_velocity
    )
    return (
        layer_output,
        input_grad,
        norm_gain_grad,
        gate_weight_grad,
        value_weight_grad,
        state_weight_grad,
        conv_value_grad,
        conv_state_grad,
        head_params_grad,
        gated_gain_grad,
        out_weight_grad,
        new_norm_gain,
        new_gate_weight,
        new_value_weight,
        new_state_weight,
        new_conv_value,
        new_conv_state,
        new_head_params,
        new_gated_gain,
        new_out_weight,
        new_norm_velocity,
        new_gate_velocity,
        new_value_velocity,
        new_state_velocity,
        new_conv_value_velocity,
        new_conv_state_velocity,
        new_head_velocity,
        new_gated_velocity,
        new_out_velocity,
    )


def solution(mesh):
    return jax.shard_map(
        body,
        mesh=mesh,
        in_specs=(
            P("seq", None),
            P("seq", None),
            P("seq"),
            P(),
            P("seq", "mp"),
            P("seq", "mp"),
            P("seq", None),
            P(),
            P(),
            P(),
            P(),
            P("seq", "mp"),
            P(),
            P("seq", "mp"),
            P("seq", "mp"),
            P("seq", None),
            P(),
            P(),
            P(),
            P(),
            P("seq", "mp"),
        ),
        out_specs=(
            P("seq", None),
            P("seq", None),
            P(),
            P("seq", "mp"),
            P("seq", "mp"),
            P("seq", None),
            P(),
            P(),
            P(),
            P(),
            P("seq", "mp"),
            P(),
            P("seq", "mp"),
            P("seq", "mp"),
            P("seq", None),
            P(),
            P(),
            P(),
            P(),
            P("seq", "mp"),
            P(),
            P("seq", "mp"),
            P("seq", "mp"),
            P("seq", None),
            P(),
            P(),
            P(),
            P(),
            P("seq", "mp"),
        ),
        check_vma=False,
    )
```

```python
import functools

import jax
import jax.numpy as jnp
from jax import lax
from jax.experimental import pallas as pl
from jax.experimental.layout import Layout, with_layout_constraint
from jax.experimental.pallas import tpu as pltpu
from jax.sharding import PartitionSpec as P

D = 1024
DI = 2048
H = 32
P_SIZE = 64
N = 128
K = 4
LANES = 128


highest = lax.Precision.HIGHEST
high = lax.Precision.HIGH
epsilon = 1e-05
momentum_decay = 0.95
matrix_rate = 0.03
vector_rate = 0.2
quintic_a = 3.4445
quintic_b = -4.775
quintic_c = 2.0315


def passed_along(shard, axis, by):
    size = lax.axis_size(axis)
    pairs = [(i, i + by) for i in range(size) if 0 <= i + by < size]
    return lax.ppermute(shard, axis, pairs)


def swapped(shard):
    return lax.ppermute(shard, "mp", [(0, 1), (1, 0)])


def pair_sum(shard):
    return shard + swapped(shard)


def exchange(array):
    return lax.all_to_all(array, "seq", 0, 0, tiled=True)


def matmul(left, right):
    return jnp.dot(left, right, precision=high)


def dot_last(left, right):
    return lax.dot_general(left, right, (((1,), (1,)), ((), ())), precision=high)


def dot_first(left, right):
    return lax.dot_general(left, right, (((0,), (0,)), ((), ())), precision=high)


def silu_slope(value):
    sigma = jax.nn.sigmoid(value)
    return sigma * (1.0 + value * (1.0 - sigma))


def carry_kernel(reverse, part_ref, out_ref):
    count, rows, _ = out_ref.shape

    def one(lap, state):
        source = count - 1 - lap if reverse else lap
        out_ref[source] = state
        return part_ref[source, rows : rows + 1] * state + part_ref[source, :rows]

    lax.fori_loop(0, count, one, jnp.zeros((rows, N), jnp.float32))


def carried_in(decay, state, reverse):
    count = lax.axis_size("seq")
    heads = state.shape[0]
    rows = heads * P_SIZE // count
    owner = jnp.repeat(decay, P_SIZE).reshape(count, rows)[:, :1]
    part = jnp.concatenate(
        [state.reshape(count, rows, N), jnp.broadcast_to(owner[:, :, None], (count, 8, N))], 1
    )
    gathered = exchange(part)
    entering = pl.pallas_call(
        functools.partial(carry_kernel, reverse),
        out_shape=jax.ShapeDtypeStruct((count, rows, N), jnp.float32),
        name="carry",
    )(gathered)
    return exchange(entering).reshape(heads, P_SIZE, N)


def chain_kernel(gram_ref, out_ref):
    count, size, _ = gram_ref.shape
    row = lax.broadcasted_iota(jnp.int32, (size, size), 0)
    col = lax.broadcasted_iota(jnp.int32, (size, size), 1)
    eye = (row == col).astype(jnp.float32)
    grams = []
    totals = []
    for unit in range(count):
        gram = gram_ref[unit]
        norm = jnp.sqrt(jnp.sum(gram * eye, keepdims=True)) + 1e-07
        grams.append(gram / (norm * norm))
        totals.append(eye / norm)
    for sweep in range(5):
        squares = [jnp.dot(gram, gram, precision=highest) for gram in grams]
        steps = [
            quintic_a * eye + quintic_b * gram + quintic_c * square
            for gram, square in zip(grams, squares)
        ]
        totals = [
            jnp.dot(total, step, precision=highest) for total, step in zip(totals, steps)
        ]
        if sweep < 4:
            halves = [
                jnp.dot(step, gram, precision=highest) for step, gram in zip(steps, grams)
            ]
            grams = [
                jnp.dot(half, step, precision=highest) for half, step in zip(halves, steps)
            ]
    for unit in range(count):
        out_ref[unit] = totals[unit]


def chain(grams):
    return pl.pallas_call(
        chain_kernel,
        out_shape=jax.ShapeDtypeStruct(grams.shape, jnp.float32),
        name="chain",
    )(grams)


def padded_to(array, multiple):
    extra = -array.shape[0] % multiple
    return jnp.pad(array, ((0, extra),) + ((0, 0),) * (array.ndim - 1))


def row_major(array):
    return with_layout_constraint(array, Layout(major_to_minor=(0, 1)))


def rows_sum(array, width):
    gathered = exchange(array)
    return jnp.sum(gathered.reshape(lax.axis_size("seq"), -1, width), 0)


def head_grams(update):
    split = update.reshape(update.shape[0], -1, P_SIZE)
    return jnp.einsum("rup,ruq->upq", split, split, precision=highest)


def apply_heads(update, polynomials):
    split = update.reshape(update.shape[0], -1, P_SIZE)
    return jnp.einsum("rup,upq->ruq", split, polynomials, precision=highest).reshape(update.shape)


def gathered_sum(grams, others):
    count = lax.axis_size("seq")
    others = padded_to(others, 8 * count)
    own_rows = others.shape[0] // count
    sent = jnp.concatenate(
        [grams.reshape(count, -1, LANES), others.reshape(count, own_rows, LANES)], 1
    )
    return jnp.sum(exchange(sent), 0), own_rows


def told_all(own, others, gram_rows, other_rows):
    count = lax.axis_size("seq")
    told = jnp.concatenate([own.reshape(gram_rows, LANES), others], 0)
    told = exchange(jnp.broadcast_to(told[None], (count,) + told.shape))
    return (
        told[:, :gram_rows].reshape(-1, P_SIZE, P_SIZE),
        told[:, gram_rows:].reshape(count * other_rows, LANES),
    )


def vector_step(current, gradient, velocity):
    new_velocity = momentum_decay * velocity + gradient
    direction = gradient + momentum_decay * new_velocity
    magnitude = jnp.sqrt(jnp.mean(current * current))
    return (
        current
        - vector_rate * magnitude * direction / jnp.sqrt(jnp.mean(direction * direction) + 1e-06),
        new_velocity,
    )


def matrix_momentum(gradient, velocity):
    new_velocity = momentum_decay * velocity + gradient
    return new_velocity, gradient + momentum_decay * new_velocity


def body(
    layer_input,
    cotangent,
    doc_starts,
    norm_gain,
    gate_weight,
    value_weight,
    state_weight,
    conv_value,
    conv_state,
    head_params,
    gated_gain,
    out_weight,
    norm_gain_velocity,
    gate_weight_velocity,
    value_weight_velocity,
    state_weight_velocity,
    conv_value_velocity,
    conv_state_velocity,
    head_params_velocity,
    gated_gain_velocity,
    out_weight_velocity,
):
    seq_count = lax.axis_size("seq")
    model_count = lax.axis_size("mp")
    model_index = lax.axis_index("mp")
    rows = layer_input.shape[0]
    inner = DI // model_count
    heads = H // model_count
    inner_start = model_index * inner
    head_start = model_index * heads
    rim = K - 1
    own_map = lax.dynamic_slice_in_dim(state_weight, model_index * N, N, 1)
    own_step = lax.dynamic_slice_in_dim(state_weight, 2 * N + head_start, heads, 1)
    mixed_full = lax.all_gather(
        jnp.concatenate([value_weight, own_map, own_step], 1), "seq", axis=0, tiled=True
    )
    outer_full = lax.all_gather(
        jnp.concatenate([gate_weight, out_weight], 1), "seq", axis=0, tiled=True
    )
    gain_local = lax.dynamic_slice_in_dim(gated_gain, inner_start, inner, 0)
    conv_local = jnp.concatenate(
        [
            lax.dynamic_slice_in_dim(conv_value, inner_start, inner, 1),
            lax.dynamic_slice_in_dim(conv_state, model_index * N, N, 1),
        ],
        1,
    )
    head_local = lax.dynamic_slice_in_dim(head_params, head_start, heads, 1)
    starts_float = doc_starts.astype(jnp.float32)
    scale = lax.rsqrt(jnp.mean(layer_input * layer_input, 1, keepdims=True) + epsilon)
    normed = layer_input * scale
    features = normed * norm_gain
    raw = jnp.dot(features, mixed_full, precision=highest)
    mixed_in = raw[:, : inner + N]
    prev_starts = passed_along(starts_float[rows - rim :], "seq", 1)
    prev_rows = passed_along(mixed_in[rows - rim :], "seq", 1)
    padded = jnp.concatenate([prev_rows, mixed_in], 0)
    cumulative = jnp.cumsum(jnp.concatenate([prev_starts, starts_float]))
    keeps = [jnp.ones((rows,), jnp.float32)]
    for lag in range(1, K):
        keeps.append(
            (cumulative[rim:] - cumulative[rim - lag : rim - lag + rows] < 0.5).astype(jnp.float32)
        )
    conv_pre = conv_local[K] + jnp.zeros_like(mixed_in)
    for lag in range(K):
        conv_pre = (
            conv_pre + keeps[lag][:, None] * conv_local[lag] * padded[rim - lag : rim - lag + rows]
        )
    activated = jax.nn.silu(conv_pre)
    head_values = activated[:, :inner].reshape(rows, heads, P_SIZE)
    this_map = activated[:, inner:]
    other_map = swapped(this_map)
    input_map = jnp.where(model_index == 0, this_map, other_map)
    read_map = jnp.where(model_index == 0, other_map, this_map)
    step_pre = raw[:, inner + N :] + head_local[0]
    step_size = jax.nn.softplus(step_pre)
    rate = -jnp.exp(head_local[1])
    skip = head_local[2]
    log_sums = jnp.cumsum(step_size * rate, 0)
    segment = jnp.cumsum(starts_float)
    position = jnp.arange(rows)
    causal_mask = (
        (position[:, None] >= position[None, :]) & (segment[:, None] == segment[None, :])
    )[None]
    head_logs = log_sums.T
    log_gap = head_logs[:, :, None] - head_logs[:, None, :]
    decay_mat = jnp.where(causal_mask, jnp.exp(jnp.where(causal_mask, log_gap, 0.0)), 0.0)
    scores = lax.dot_general(read_map, input_map, (((1,), (1,)), ((), ())), precision=highest)
    weighted = decay_mat * scores[None]
    scaled = head_values * step_size[..., None]
    last_log = log_sums[-1]
    last_segment = segment[-1]
    tail_weight = jnp.exp(last_log[None] - log_sums) * (segment == last_segment)[:, None]
    tail_scaled = scaled * tail_weight[..., None]
    block_state = jnp.einsum("jhp,jn->hpn", tail_scaled, input_map, precision=highest)
    block_decay = jnp.exp(last_log) * (last_segment == 0)
    entry_weight = jnp.exp(log_sums) * (segment == 0)[:, None]
    entries = carried_in(block_decay, block_state, False)
    intra = jnp.einsum("hij,jhp->ihp", weighted, scaled, precision=highest)
    state_read = jnp.einsum("hpn,in->ihp", entries, read_map, precision=highest)
    ssd_out = (
        intra + entry_weight[..., None] * state_read + head_values * skip[None, :, None]
    ).reshape(rows, inner)
    gate_full = outer_full[:, :inner]
    out_full = outer_full[:, inner:]
    gate = matmul(features, gate_full)
    grad_gated = matmul(cotangent, out_full)
    grad_hat = grad_gated * gain_local
    gate_act = jax.nn.silu(gate)
    product = ssd_out * gate_act
    row_sums = pair_sum(jnp.stack([jnp.sum(product * product, 1), jnp.sum(product * grad_hat, 1)]))
    gate_scale = lax.rsqrt(row_sums[0] / DI + epsilon)[:, None]
    inner_sum = row_sums[1][:, None]
    gated = product * gate_scale * gain_local
    grad_product = gate_scale * (grad_hat - product * gate_scale * gate_scale * (inner_sum / DI))
    grad_gate = grad_product * ssd_out * silu_slope(gate)
    early = 5 * inner // 8
    outer_partial = jnp.concatenate(
        [
            row_major(dot_first(features, grad_gate)),
            row_major(dot_first(cotangent, gated[:, :early])),
        ],
        1,
    )
    outer_partial, grad_product = lax.optimization_barrier((outer_partial, grad_product))
    outer_reduced = lax.psum_scatter(outer_partial, "seq", scatter_dimension=0, tiled=True)
    layer_output = layer_input + pair_sum(dot_last(gated, out_full))
    gated_gain_part = jnp.sum(grad_gated * product * gate_scale, 0)
    ssd_grad = (grad_product * gate_act).reshape(rows, heads, P_SIZE)
    skip_grad = jnp.sum(ssd_grad * head_values, (0, 2))
    weighted_grad = ssd_grad * entry_weight[..., None]
    enter_grad = jnp.einsum("ihp,in->hpn", weighted_grad, read_map, precision=highest)
    out_grads = carried_in(block_decay, enter_grad, True)
    late_partial = row_major(dot_first(cotangent, gated[:, early:]))
    late_partial, out_grads = lax.optimization_barrier((late_partial, out_grads))
    late_reduced = rows_sum(late_partial, inner - early)
    read_grad = jnp.einsum("ihp,hpn->in", weighted_grad, entries, precision=highest)
    logs_grad = jnp.sum(ssd_grad * state_read, 2) * entry_weight
    mix_grad = jnp.einsum("ihp,jhp->hij", ssd_grad, scaled, precision=highest)
    scaled_grad = jnp.einsum("hij,ihp->jhp", weighted, ssd_grad, precision=highest)
    score_grad = jnp.sum(mix_grad * decay_mat, 0)
    read_grad = read_grad + jnp.dot(score_grad, input_map, precision=highest)
    input_grad_map = lax.dot_general(
        score_grad, read_map, (((0,), (0,)), ((), ())), precision=highest
    )
    decay_term = mix_grad * weighted
    logs_grad = logs_grad + (jnp.sum(decay_term, 2) - jnp.sum(decay_term, 1)).T
    from_state = jnp.einsum("hpn,jn->jhp", out_grads, input_map, precision=highest)
    scaled_grad = scaled_grad + tail_weight[..., None] * from_state
    input_grad_map = input_grad_map + jnp.einsum(
        "hpn,jhp->jn", out_grads, tail_scaled, precision=highest
    )
    tail_grad = jnp.sum(from_state * tail_scaled, 2)
    last_grad = jnp.sum(tail_grad, 0) + jnp.sum(out_grads * entries, (1, 2)) * block_decay
    logs_grad = logs_grad - tail_grad
    onward = (position[:, None] <= position[None, :]).astype(jnp.float32)
    decay_log_grad = jnp.dot(onward, logs_grad, precision=highest) + last_grad[None]
    grad_values = ssd_grad * skip[None, :, None] + scaled_grad * step_size[..., None]
    step_grad = jnp.sum(scaled_grad * head_values, 2) + decay_log_grad * rate
    rate_grad = jnp.sum(decay_log_grad * step_size, 0)
    log_rate_grad = rate_grad * rate
    step_pre_grad = step_grad * jax.nn.sigmoid(step_pre)
    bias_grad = jnp.sum(step_pre_grad, 0)
    this_grad = jnp.where(model_index == 0, input_grad_map, read_grad)
    other_grad = jnp.where(model_index == 0, read_grad, input_grad_map)
    act_grad = jnp.concatenate(
        [grad_values.reshape(rows, inner), this_grad + swapped(other_grad)], 1
    )
    pre_grad = act_grad * silu_slope(conv_pre)
    conv_rows = []
    padded_grad = jnp.zeros_like(padded)
    for lag in range(K):
        masked = keeps[lag][:, None] * pre_grad
        conv_rows.append(jnp.sum(masked * padded[rim - lag : rim - lag + rows], 0))
        padded_grad = padded_grad + jnp.pad(masked * conv_local[lag], ((rim - lag, lag), (0, 0)))
    conv_rows.append(jnp.sum(pre_grad, 0))
    conv_local_grad = jnp.stack(conv_rows)
    spill = passed_along(padded_grad[:rim], "seq", -1)
    mixed_grad = padded_grad[rim:] + jnp.pad(spill, ((rows - rim, 0), (0, 0)))
    raw_grad = jnp.concatenate([mixed_grad, step_pre_grad], 1)
    mixed_partial = row_major(dot_first(features, mixed_grad[:, :inner]))
    map_partial = row_major(dot_first(features, mixed_grad[:, inner:]))
    step_partial = dot_first(features, step_pre_grad)
    mixed_partial, raw_grad, map_partial = lax.optimization_barrier(
        (mixed_partial, raw_grad, map_partial)
    )
    step_rows = D * heads // LANES // seq_count
    state_sums = rows_sum(
        jnp.concatenate(
            [
                map_partial.reshape(seq_count, -1, LANES),
                step_partial.reshape(seq_count, step_rows, LANES),
            ],
            1,
        ),
        LANES,
    )
    raw_grad, late_reduced, state_sums = lax.optimization_barrier(
        (raw_grad, late_reduced, state_sums)
    )
    mixed_reduced = lax.psum_scatter(mixed_partial, "seq", scatter_dimension=0, tiled=True)
    features_grad = pair_sum(dot_last(grad_gate, gate_full) + dot_last(raw_grad, mixed_full))
    norm_gain_part = jnp.sum(features_grad * normed, 0)
    gain_grad_in = features_grad * norm_gain
    input_grad = cotangent + scale * (
        gain_grad_in - normed * jnp.mean(gain_grad_in * normed, 1, keepdims=True)
    )

    factor = matrix_rate * 0.2 * D**0.5
    gate_weight_grad = outer_reduced[:, :inner]
    out_weight_grad = jnp.concatenate([outer_reduced[:, inner:], late_reduced], 1)
    new_gate_velocity, gate_update = matrix_momentum(gate_weight_grad, gate_weight_velocity)
    new_out_velocity, out_update = matrix_momentum(out_weight_grad, out_weight_velocity)
    outer_update = jnp.concatenate([gate_update, out_update], 1)
    outer_grams = padded_to(head_grams(outer_update), seq_count)
    per = outer_grams.shape[0] // seq_count
    outer_rows = per * P_SIZE * P_SIZE // LANES
    this_state = jnp.concatenate(
        [state_sums[:-step_rows], state_sums[-step_rows:].reshape(-1, heads)], 1
    )
    other_state = swapped(this_state)
    first = jnp.where(model_index == 0, this_state, other_state)
    second = jnp.where(model_index == 0, other_state, this_state)
    state_weight_grad = jnp.concatenate(
        [first[:, :N], second[:, :N], first[:, N:], second[:, N:]], 1
    )
    new_state_velocity, state_update = matrix_momentum(state_weight_grad, state_weight_velocity)
    map_update = state_update[:, : 2 * N].reshape(-1, 2, N)
    step_update = state_update[:, 2 * N :]
    map_grams = jnp.einsum("rup,ruq->upq", map_update, map_update, precision=highest)
    step_gram = lax.dot_general(
        step_update, step_update, (((0,), (0,)), ((), ())), precision=highest
    )
    others = jnp.concatenate(
        [
            map_grams.reshape(2 * N, N),
            jnp.pad(step_gram, ((0, 0), (0, N - H))),
            norm_gain_part.reshape(-1, LANES),
            conv_local_grad.reshape(-1, LANES),
            gated_gain_part.reshape(-1, LANES),
            jnp.pad(jnp.stack([bias_grad, log_rate_grad, skip_grad]), ((0, 0), (0, LANES - heads))),
        ],
        0,
    )
    summed, other_rows = gathered_sum(outer_grams, others)
    outer_own = chain(summed[:outer_rows].reshape(per, P_SIZE, P_SIZE))
    outer_poly, others = told_all(outer_own, summed[outer_rows:], outer_rows, other_rows)
    mixed_reduced, outer_poly = lax.optimization_barrier((mixed_reduced, outer_poly))
    outer_orth = apply_heads(outer_update, outer_poly[: 2 * heads])
    new_gate_weight = gate_weight - factor * outer_orth[:, :inner]
    new_out_weight = out_weight - factor * outer_orth[:, inner:]
    state_poly = chain(
        jnp.stack(
            [
                others[:N],
                others[N : 2 * N],
                jnp.pad(others[2 * N : 2 * N + H], ((0, N - H), (0, 0))),
            ]
        )
    )
    state_orth = jnp.concatenate(
        [
            jnp.einsum("rup,upq->ruq", map_update, state_poly[:2], precision=highest).reshape(
                -1, 2 * N
            ),
            jnp.dot(step_update, state_poly[2, :H, :H], precision=highest),
        ],
        1,
    )
    new_state_weight = state_weight - factor * state_orth

    vectors = others[2 * N + H :]
    at = D // LANES
    norm_gain_grad = vectors[:at].reshape(D)
    other = swapped(vectors)
    first = jnp.where(model_index == 0, vectors, other)
    second = jnp.where(model_index == 0, other, vectors)
    conv_rows = (K + 1) * (inner + N) // LANES
    conv_first, conv_second = (
        side[at : at + conv_rows].reshape(K + 1, inner + N) for side in (first, second)
    )
    conv_value_grad = jnp.concatenate([conv_first[:, :inner], conv_second[:, :inner]], 1)
    conv_state_grad = jnp.concatenate([conv_first[:, inner:], conv_second[:, inner:]], 1)
    at = at + conv_rows
    gated_rows = inner // LANES
    gated_gain_grad = jnp.concatenate(
        [first[at : at + gated_rows].reshape(inner), second[at : at + gated_rows].reshape(inner)]
    )
    at = at + gated_rows
    head_params_grad = jnp.concatenate(
        [first[at : at + 3, :heads], second[at : at + 3, :heads]], 1
    )

    value_weight_grad = mixed_reduced
    new_value_velocity, value_update = matrix_momentum(value_weight_grad, value_weight_velocity)
    value_grams = padded_to(head_grams(value_update), seq_count)
    per = value_grams.shape[0] // seq_count
    value_rows = per * P_SIZE * P_SIZE // LANES
    summed = jnp.sum(exchange(value_grams.reshape(seq_count, value_rows, LANES)), 0)
    value_own = chain(summed.reshape(per, P_SIZE, P_SIZE)).reshape(value_rows, LANES)
    told = exchange(jnp.broadcast_to(value_own[None], (seq_count, value_rows, LANES)))
    value_poly = told.reshape(-1, P_SIZE, P_SIZE)[:heads]
    value_orth = apply_heads(value_update, value_poly)
    new_value_weight = value_weight - factor * value_orth

    new_norm_gain, new_norm_velocity = vector_step(norm_gain, norm_gain_grad, norm_gain_velocity)
    new_conv_value, new_conv_value_velocity = vector_step(
        conv_value, conv_value_grad, conv_value_velocity
    )
    new_conv_state, new_conv_state_velocity = vector_step(
        conv_state, conv_state_grad, conv_state_velocity
    )
    new_head_params, new_head_velocity = vector_step(
        head_params, head_params_grad, head_params_velocity
    )
    new_gated_gain, new_gated_velocity = vector_step(
        gated_gain, gated_gain_grad, gated_gain_velocity
    )
    return (
        layer_output,
        input_grad,
        norm_gain_grad,
        gate_weight_grad,
        value_weight_grad,
        state_weight_grad,
        conv_value_grad,
        conv_state_grad,
        head_params_grad,
        gated_gain_grad,
        out_weight_grad,
        new_norm_gain,
        new_gate_weight,
        new_value_weight,
        new_state_weight,
        new_conv_value,
        new_conv_state,
        new_head_params,
        new_gated_gain,
        new_out_weight,
        new_norm_velocity,
        new_gate_velocity,
        new_value_velocity,
        new_state_velocity,
        new_conv_value_velocity,
        new_conv_state_velocity,
        new_head_velocity,
        new_gated_velocity,
        new_out_velocity,
    )


def solution(mesh):
    return jax.shard_map(
        body,
        mesh=mesh,
        in_specs=(
            P("seq", None),
            P("seq", None),
            P("seq"),
            P(),
            P("seq", "mp"),
            P("seq", "mp"),
            P("seq", None),
            P(),
            P(),
            P(),
            P(),
            P("seq", "mp"),
            P(),
            P("seq", "mp"),
            P("seq", "mp"),
            P("seq", None),
            P(),
            P(),
            P(),
            P(),
            P("seq", "mp"),
        ),
        out_specs=(
            P("seq", None),
            P("seq", None),
            P(),
            P("seq", "mp"),
            P("seq", "mp"),
            P("seq", None),
            P(),
            P(),
            P(),
            P(),
            P("seq", "mp"),
            P(),
            P("seq", "mp"),
            P("seq", "mp"),
            P("seq", None),
            P(),
            P(),
            P(),
            P(),
            P("seq", "mp"),
            P(),
            P("seq", "mp"),
            P("seq", "mp"),
            P("seq", None),
            P(),
            P(),
            P(),
            P(),
            P("seq", "mp"),
        ),
        check_vma=False,
    )
```
